32 devices in a mesh: dom: 16 (over z, y, core), dest: 2 (over x).
Axes of the slice: x: 2, y: 2, z: 4, core: 2. Of those that a mesh axis runs over, the one named last changes fastest.
Arguments:
- features: bfloat16 [65536, 128], P('dom')
- w_input: bfloat16 [128, 512], replicated, may hold values from -0.5 to 0.5
- b_input: float32 [512], replicated, may hold values from -3 to 3
- w_output: float32 [512], replicated, may hold values from -0.25 to 0.25
- terminal: float32 [32, 65536], P('dest', 'dom'), may hold values from -4 to 4
- start_counts: int32 [32, 65536], P('dest', 'dom'), may hold values from 0 to 3
- visit_counts: int32 [32, 65536], P('dest', 'dom'), may hold values from 0 to 3
- dest_nodes: int32 [32], P('dest'), may hold values from 0 to 65535
- tile_rows: int32 [1280], P('dom'), may hold values from 0 to 31, as said below
- tile_cols: int32 [1280], P('dom'), may hold values from 0 to 47, as said below
- send_blocks: int32 [128, 2], P('dom'), may hold values from 0 to 31
- tile_weight: bfloat16 [1280, 128, 128], P('dom'), as said below
Outputs:
- values: float32 [32, 65536], P('dest', 'dom')
- grad_w_input: float32 [128, 512], replicated
- grad_b_input: float32 [512], replicated
- grad_w_output: float32 [512], replicated
The draws below stay inside these ranges and needn't reach their ends.
Inputs may be any that keep to these rules, and one draw needn't show every extreme that they name: `tile_rows`: the first 32 tiles of every partition are its diagonal tiles, in order. `tile_cols`: the first 32 tiles of a partition have columns 0 .. 31 in order. A column of 32 or more names a slot of a neighbour q = p - f that exists; every slot of every existing neighbour is named by exactly one tile. `tile_weight`: every entry is zero or positive; every row of a diagonal tile has a positive entry.
All inputs are finite; a program needn't handle non-finite values.
Results may differ from the reference program's by a relative error of at most 0.0003.
Values sent between devices are 32-bit elements; how exact they have to be, the bound alone decides.
No kernel may reach another device: no remote copies, remote signals or barrier semaphores. Data moves between devices by JAX's collectives and lax.ppermute only.
A program may use at most 64 MiB of HBM per device.

```python
import math
import jax
import jax.numpy as jnp
from jax import lax

BLK = 128
BLOCKS_DEV = 32
LOCAL_TILES = 2
REACH = 4
SLOTS_PEER = 2
TILES_DEV = 80
NODES = 65536
DEST = 32
FEAT = 128
HID = 512
STEPS = 3
N_DOM = 16


def tile_layout(key):
    base_key = jax.random.fold_in(key, 7)
    key_rows, key_remote, key_cols, key_spare = jax.random.split(base_key, 4)
    slot_count = 2 * REACH * SLOTS_PEER
    devices = jnp.arange(N_DOM, dtype=jnp.int32)[:, None]
    diagonal = jnp.broadcast_to(jnp.arange(BLOCKS_DEV, dtype=jnp.int32)[None, :], (N_DOM, BLOCKS_DEV))
    extra_rows = jax.random.randint(key_rows, (N_DOM, BLOCKS_DEV * (LOCAL_TILES - 1)), 0, BLOCKS_DEV, dtype=jnp.int32)
    remote_rows = jax.random.randint(key_remote, (N_DOM, slot_count), 0, BLOCKS_DEV, dtype=jnp.int32)
    extra_cols = jax.random.randint(key_cols, (N_DOM, BLOCKS_DEV * (LOCAL_TILES - 1)), 0, BLOCKS_DEV, dtype=jnp.int32)
    spare_cols = jax.random.randint(key_spare, (N_DOM, slot_count), 0, BLOCKS_DEV, dtype=jnp.int32)
    position = jnp.arange(slot_count, dtype=jnp.int32) // SLOTS_PEER
    offset = jnp.where(position < REACH, position - REACH, position - REACH + 1)
    sender = devices - offset[None, :]
    present = (sender >= 0) & (sender < N_DOM)
    remote_cols = jnp.where(present, BLOCKS_DEV + jnp.arange(slot_count, dtype=jnp.int32)[None, :], spare_cols)
    row_list = jnp.concatenate([diagonal, extra_rows, remote_rows], axis=1)
    col_list = jnp.concatenate([diagonal, extra_cols, remote_cols], axis=1)
    return (row_list.reshape(-1), col_list.reshape(-1))


def draw_tile_rows(key, part):
    return tile_layout(key)[0]


def draw_tile_cols(key, part):
    return tile_layout(key)[1]


def draw_tile_weight(key, part):
    key_shift, key_mask, key_cycle, key_sparse = jax.random.split(jax.random.fold_in(key, 3), 4)
    tile_count = N_DOM * TILES_DEV
    shape = (tile_count, BLK, BLK)
    shifts = jax.random.randint(key_shift, (tile_count, 1, 1), 0, BLK, dtype=jnp.int32)
    row_ids = jnp.arange(BLK, dtype=jnp.int32)[None, :, None]
    col_ids = jnp.arange(BLK, dtype=jnp.int32)[None, None, :]
    on_cycle = (col_ids == (row_ids + shifts) % BLK).astype(jnp.float32)
    linked = (jax.random.uniform(key_mask, shape, jnp.float32) < 4.0 / BLK).astype(jnp.float32)
    cycle_weight = jax.random.uniform(key_cycle, (tile_count, BLK, 1), jnp.float32, 1.0, 3.0)
    sparse_weight = jax.random.uniform(key_sparse, shape, jnp.float32, 0.2, 1.8)
    entries = on_cycle * cycle_weight + linked * sparse_weight
    return (entries / (6.0 * (LOCAL_TILES + 1))).astype(jnp.bfloat16)


def draw_terminal(key, part):
    key_base, key_spot = jax.random.split(jax.random.fold_in(key, 11), 2)
    block_count = NODES // BLK
    spots = jax.random.randint(key_spot, (DEST, block_count, 1), 0, BLK, dtype=jnp.int32)
    within = jnp.arange(BLK, dtype=jnp.int32)[None, None, :]
    peak = (within == spots).astype(jnp.float32)
    base = -3.0 + jnp.clip(0.3 * jax.random.normal(key_base, (DEST, block_count, BLK), jnp.float32), -1.0, 1.0)
    height = jnp.full((DEST, block_count, 1), 6.0, jnp.float32)
    return (base + peak * height).reshape(DEST, NODES)


def draw_features(key, part):
    key_main = jax.random.fold_in(jax.random.fold_in(key, 5), 0)
    rising = 1.0 + 2.0 * jnp.arange(NODES, dtype=jnp.float32)[:, None] / NODES
    entries = jax.random.normal(key_main, (NODES, FEAT), jnp.float32) * rising
    return entries.astype(jnp.bfloat16)


def touch_ends(drawn, own_key, smallest, top_value):
    shape = drawn.shape
    spot = [jax.random.randint(jax.random.fold_in(own_key, axis), (), 0, shape[axis]) for axis in range(len(shape))]
    drawn = drawn.at[tuple(spot)].set(smallest)
    longest = shape.index(max(shape))
    spot[longest] = (spot[longest] + 1) % shape[longest]
    return drawn.at[tuple(spot)].set(top_value)


def gaussian(rng, dims, scale, most, held_as=jnp.bfloat16):
    values = jax.random.normal(rng, dims, jnp.float32) * scale
    return jnp.minimum(jnp.maximum(values, -most), most).astype(held_as)


def setup_inputs(seed: int = 0) -> dict:
    key_of = jax.random.split(jax.random.key(seed), 13)
    features = draw_features(jax.random.fold_in(key_of[12], 71), 0)
    w_input = gaussian(key_of[1], (FEAT, HID), FEAT ** -0.5, 0.5)
    b_input = gaussian(key_of[2], (HID,), 0.5, 3.0, jnp.float32)
    w_output = gaussian(key_of[3], (HID,), HID ** -0.5, 0.25, jnp.float32)
    terminal = draw_terminal(jax.random.fold_in(key_of[12], 71), 0)
    start_counts = touch_ends(jax.random.randint(key_of[5], (DEST, NODES), 0, 4), jax.random.fold_in(key_of[5], 1), 0, 3).astype(jnp.int32)
    visit_counts = touch_ends(jax.random.randint(key_of[6], (DEST, NODES), 0, 4), jax.random.fold_in(key_of[6], 1), 0, 3).astype(jnp.int32)
    dest_nodes = touch_ends(jax.random.randint(key_of[7], (DEST,), 0, NODES), jax.random.fold_in(key_of[7], 1), 0, NODES - 1).astype(jnp.int32)
    tile_rows = draw_tile_rows(jax.random.fold_in(key_of[12], 71), 0)
    tile_cols = draw_tile_cols(jax.random.fold_in(key_of[12], 71), 0)
    send_blocks = touch_ends(jax.random.randint(key_of[10], (N_DOM * 2 * REACH, SLOTS_PEER), 0, BLOCKS_DEV), jax.random.fold_in(key_of[10], 1), 0, BLOCKS_DEV - 1).astype(jnp.int32)
    tile_weight = draw_tile_weight(jax.random.fold_in(key_of[12], 71), 0)
    return dict(features=features, w_input=w_input, b_input=b_input, w_output=w_output, terminal=terminal, start_counts=start_counts, visit_counts=visit_counts, dest_nodes=dest_nodes, tile_rows=tile_rows, tile_cols=tile_cols, send_blocks=send_blocks, tile_weight=tile_weight)


goal_gain = 32.0

def peer_offsets():
    return jnp.array([o - REACH if o < REACH else o - REACH + 1 for o in range(2 * REACH)], jnp.int32)

def reference(features, w_input, b_input, w_output, terminal, start_counts, visit_counts, dest_nodes, tile_rows, tile_cols, send_blocks, tile_weight):
    hp = lax.Precision.HIGHEST
    all_blocks = N_DOM * BLOCKS_DEV
    hidden_pre = jnp.dot(features, w_input, preferred_element_type=jnp.float32) + b_input
    activation = jnp.tanh(hidden_pre)
    reward = jnp.dot(activation, w_output, precision=hp)
    growth = jnp.exp(reward).reshape(all_blocks, BLK)
    row_list = tile_rows.reshape(N_DOM, TILES_DEV)
    col_list = tile_cols.reshape(N_DOM, TILES_DEV)
    devices = jnp.arange(N_DOM, dtype=jnp.int32)[:, None]
    global_rows = devices * BLOCKS_DEV + row_list
    slot_index = jnp.clip(col_list - BLOCKS_DEV, 0, 2 * REACH * SLOTS_PEER - 1)
    position = slot_index // SLOTS_PEER
    within = slot_index % SLOTS_PEER
    sender = jnp.clip(devices - peer_offsets()[position], 0, N_DOM - 1)
    send_table = send_blocks.reshape(N_DOM, 2 * REACH, SLOTS_PEER)
    remote = sender * BLOCKS_DEV + send_table[sender, position, within]
    global_cols = jnp.where(col_list < BLOCKS_DEV, devices * BLOCKS_DEV + col_list, remote).astype(jnp.int32)
    tiles = tile_weight.reshape(N_DOM, TILES_DEV, BLK, BLK)
    goal_mask = goal_gain * (jnp.arange(NODES, dtype=jnp.int32)[None, :] == dest_nodes[:, None]).astype(jnp.float32).reshape(DEST, all_blocks, BLK)

    def backup(field):

        def one(device):
            tile_data = tiles[device].astype(jnp.float32)
            gathered = field[:, global_cols[device], :]
            contrib = jnp.einsum('dtb,tab->dta', gathered, tile_data, precision=hp)
            return jax.ops.segment_sum(jnp.moveaxis(contrib, 1, 0), row_list[device], num_segments=BLOCKS_DEV)
        pieces = lax.map(one, jnp.arange(N_DOM, dtype=jnp.int32))
        summed = pieces.reshape(all_blocks, DEST, BLK).transpose(1, 0, 2)
        return growth[None] * summed + goal_mask

    def spread(outflow):

        def one(device):
            tile_data = tiles[device].astype(jnp.float32)
            gathered = outflow[:, global_rows[device], :]
            contrib = jnp.einsum('dta,tab->dtb', gathered, tile_data, precision=hp)
            return jnp.moveaxis(contrib, 1, 0)
        pieces = lax.map(one, jnp.arange(N_DOM, dtype=jnp.int32))
        totals = jax.ops.segment_sum(pieces.reshape(-1, DEST, BLK), global_cols.reshape(-1), num_segments=all_blocks)
        return totals.transpose(1, 0, 2)
    partition = [jnp.exp(terminal).reshape(DEST, all_blocks, BLK)]
    for step in range(STEPS):
        partition.append(backup(partition[-1]))
    values = jnp.log(partition[STEPS]).reshape(DEST, NODES)
    visits_now = start_counts.astype(jnp.float32).reshape(DEST, all_blocks, BLK)
    expected = jnp.zeros((DEST, all_blocks, BLK), jnp.float32)
    for step in range(STEPS):
        outflow = growth[None] * visits_now / partition[STEPS - step]
        visits_now = partition[STEPS - 1 - step] * spread(outflow)
        expected = expected + visits_now
    node_grad = lax.optimization_barrier(jnp.sum(visit_counts.astype(jnp.float32) - expected.reshape(DEST, NODES), axis=0)) / math.sqrt(NODES * DEST)
    grad_w_output = jnp.dot(node_grad, activation, precision=hp)
    pre_grad = node_grad[:, None] * w_output[None, :] * (1.0 - activation * activation)
    grad_w_input = jnp.dot(features.astype(jnp.float32).T, pre_grad, precision=hp)
    grad_b_input = lax.optimization_barrier(jnp.sum(pre_grad, axis=0))
    return (values, grad_w_input, grad_b_input, grad_w_output)
```

```python
import functools
import math

import jax
import jax.numpy as jnp
from jax import lax
from jax.experimental import pallas as pl
from jax.experimental.pallas import tpu as pltpu
from jax.sharding import PartitionSpec as P

STEPS = 3
GOAL_GAIN = 32.0
VMEM_GRANT = 24 << 20

NT = (((1,), (1,)), ((), ()))
NN = (((1,), (0,)), ((), ()))


def offset_of(o, reach):
    return o - reach if o < reach else o - reach + 1


def neighbour(me, count, shift):
    there = me + shift
    present = jnp.logical_and(there >= 0, there < count)
    return present, jnp.where(present, there, me)


def call(kernel, out_shape, scratch, ins, smem, flops, moved):
    return pl.pallas_call(
        kernel,
        out_shape=out_shape,
        in_specs=[pl.BlockSpec(memory_space=pltpu.SMEM)] * smem
        + [pl.BlockSpec(memory_space=pltpu.VMEM)] * (len(ins) - smem),
        out_specs=jax.tree.map(lambda _: pl.BlockSpec(memory_space=pltpu.VMEM), out_shape),
        scratch_shapes=scratch,
        compiler_params=pltpu.CompilerParams(vmem_limit_bytes=VMEM_GRANT),
        cost_estimate=pl.CostEstimate(flops=flops, bytes_accessed=moved, transcendentals=0),
    )(*ins)


def store_split(ref, k, x):
    rows = x.shape[0]
    high = x.astype(jnp.bfloat16)
    low = (x - high.astype(jnp.float32)).astype(jnp.bfloat16)
    ref[k, :rows] = high
    ref[k, rows:] = low


def product(lhs, rhs, dims):
    both = lax.dot_general(lhs, rhs, dims, preferred_element_type=jnp.float32)
    rows = both.shape[0] // 2
    return both[:rows] + both[rows:]


def pack(out_ref, me, count, reach, width, sign, block):
    rows = None
    for o in range(2 * reach):
        _, there = neighbour(me, count, sign * offset_of(o, reach))
        for m in range(width):
            piece = block(o, m)
            rows = piece.shape[0]
            out_ref[there, m * rows : (m + 1) * rows] = piece


def network_kernel(w_ref, b_ref, v_ref, f_ref, act_ref, growth_ref):
    chunk = 512
    w = w_ref[...]
    b = b_ref[...]
    v = v_ref[...]
    for c in range(f_ref.shape[0] // chunk):
        pre = lax.dot_general(
            w, f_ref[c * chunk : (c + 1) * chunk], NT, preferred_element_type=jnp.float32
        )
        act = jnp.tanh(pre + b)
        act_ref[:, c * chunk : (c + 1) * chunk] = act
        grown = jnp.exp(jnp.sum(act * v, axis=0, keepdims=True))
        for k in range(chunk // 128):
            growth_ref[c * (chunk // 128) + k] = grown[:, k * 128 : (k + 1) * 128]


def first_kernel(count, reach, width, send_ref, term_ref, z_ref, out_ref):
    blocks = z_ref.shape[0]
    lanes = z_ref.shape[2]
    me = lax.axis_index("dom")
    for k in range(blocks):
        z_ref[k] = jnp.exp(term_ref[:, k * lanes : (k + 1) * lanes])
    pack(out_ref, me, count, reach, width, 1, lambda o, m: z_ref[send_ref[o, m]])


def gather_split(count, reach, width, z_ref, got_ref, split_ref):
    blocks, rows, _ = z_ref.shape
    me = lax.axis_index("dom")
    for k in range(blocks):
        store_split(split_ref, k, z_ref[k])
    for o in range(2 * reach):
        _, there = neighbour(me, count, -offset_of(o, reach))
        for m in range(width):
            store_split(
                split_ref, blocks + o * width + m, got_ref[there, m * rows : (m + 1) * rows]
            )


def backed_up(rows_ref, cols_ref, w_ref, split_ref, sum_ref, blocks):
    for k in range(blocks):
        sum_ref[k] = product(split_ref[k], w_ref[k], NT)
    for t in range(blocks, w_ref.shape[0]):
        r = rows_ref[t]
        sum_ref[r] = sum_ref[r] + product(split_ref[cols_ref[t]], w_ref[t], NT)


def with_goal(k, growth_ref, sum_ref, dest, me):
    blocks, rows, lanes = sum_ref.shape
    node = (me * blocks + k) * lanes + lax.broadcasted_iota(jnp.int32, (rows, lanes), 1)
    return growth_ref[k] * sum_ref[k] + jnp.where(node == dest, GOAL_GAIN, 0.0)


def backup_kernel(
    count, reach, width, rows_ref, cols_ref, send_ref, w_ref, z_ref, got_ref, growth_ref, dest_ref,
    next_ref, out_ref, split_ref, sum_ref,
):
    blocks = z_ref.shape[0]
    me = lax.axis_index("dom")
    gather_split(count, reach, width, z_ref, got_ref, split_ref)
    backed_up(rows_ref, cols_ref, w_ref, split_ref, sum_ref, blocks)
    dest = jnp.broadcast_to(dest_ref[...], sum_ref.shape[1:])
    for k in range(blocks):
        next_ref[k] = with_goal(k, growth_ref, sum_ref, dest, me)
    pack(out_ref, me, count, reach, width, 1, lambda o, m: next_ref[send_ref[o, m]])


def spread_out(rows_ref, cols_ref, w_ref, split_ref, ext_ref, blocks):
    slots = ext_ref.shape[0] - blocks
    for k in range(slots):
        ext_ref[blocks + k] = jnp.zeros(ext_ref.shape[1:], jnp.float32)
    for k in range(blocks):
        ext_ref[k] = product(split_ref[k], w_ref[k], NN)
    for t in range(blocks, w_ref.shape[0]):
        c = cols_ref[t]
        ext_ref[c] = ext_ref[c] + product(split_ref[rows_ref[t]], w_ref[t], NN)


def turn_kernel(
    count, reach, width, rows_ref, cols_ref, w_ref, z_ref, got_ref, growth_ref, dest_ref, start_ref,
    values_ref, local_ref, out_ref, split_ref, sum_ref, ext_ref,
):
    blocks, rows, lanes = z_ref.shape
    me = lax.axis_index("dom")
    gather_split(count, reach, width, z_ref, got_ref, split_ref)
    backed_up(rows_ref, cols_ref, w_ref, split_ref, sum_ref, blocks)
    dest = jnp.broadcast_to(dest_ref[...], (rows, lanes))
    for k in range(blocks):
        z = with_goal(k, growth_ref, sum_ref, dest, me)
        span = slice(k * lanes, (k + 1) * lanes)
        values_ref[:, span] = jnp.log(z)
        store_split(split_ref, k, growth_ref[k] * start_ref[:, span].astype(jnp.float32) / z)
    spread_out(rows_ref, cols_ref, w_ref, split_ref, ext_ref, blocks)
    for k in range(blocks):
        local_ref[k] = ext_ref[k]
    pack(out_ref, me, count, reach, width, -1, lambda o, m: ext_ref[blocks + o * width + m])


def take_returned(count, reach, width, send_ref, got_ref, into_ref):
    rows = into_ref.shape[1]
    me = lax.axis_index("dom")
    for o in range(2 * reach):
        present, there = neighbour(me, count, offset_of(o, reach))
        for m in range(width):
            piece = got_ref[there, m * rows : (m + 1) * rows]
            b = send_ref[o, m]
            into_ref[b] = into_ref[b] + jnp.where(present, piece, 0.0)


def spread_kernel(
    count, reach, width, rows_ref, cols_ref, send_ref, w_ref, flow_ref, got_ref, growth_ref,
    full_ref, local_ref, out_ref, split_ref, ext_ref,
):
    blocks = flow_ref.shape[0]
    me = lax.axis_index("dom")
    full_ref[...] = flow_ref[...]
    take_returned(count, reach, width, send_ref, got_ref, full_ref)
    for k in range(blocks):
        store_split(split_ref, k, growth_ref[k] * full_ref[k])
    spread_out(rows_ref, cols_ref, w_ref, split_ref, ext_ref, blocks)
    for k in range(blocks):
        local_ref[k] = ext_ref[k]
    pack(out_ref, me, count, reach, width, -1, lambda o, m: ext_ref[blocks + o * width + m])


def last_kernel(
    count, reach, width, rows_ref, cols_ref, send_ref, w_ref, flow_ref, got_ref, growth_ref,
    z0_ref, z1_ref, z2_ref, first_ref, visit_ref, far_ref,
    node_ref, out_ref, split_ref, ext_ref, full_ref,
):
    blocks, rows, lanes = flow_ref.shape
    me = lax.axis_index("dom")
    full_ref[...] = flow_ref[...]
    take_returned(count, reach, width, send_ref, got_ref, full_ref)
    for k in range(blocks):
        store_split(split_ref, k, growth_ref[k] * full_ref[k])
    spread_out(rows_ref, cols_ref, w_ref, split_ref, ext_ref, blocks)
    for k in range(blocks):
        left = (
            visit_ref[:, k * lanes : (k + 1) * lanes].astype(jnp.float32)
            - z2_ref[k] * first_ref[k]
            - z1_ref[k] * full_ref[k]
            - z0_ref[k] * ext_ref[k]
        )
        node_ref[k] = jnp.sum(left, axis=0, keepdims=True)

    for o in range(2 * reach):
        _, back = neighbour(me, count, -offset_of(o, reach))
        pieces = [
            jnp.sum(
                far_ref[back, m * rows : (m + 1) * rows] * ext_ref[blocks + o * width + m],
                axis=0,
                keepdims=True,
            )
            for m in range(width)
        ]
        out_ref[back] = jnp.concatenate(
            pieces + [jnp.zeros((8 - width, lanes), jnp.float32)], axis=0
        )


def gradient_kernel(
    count, reach, width, scale, send_ref, v_ref, f_ref, act_ref, node_ref, got_ref,
    grad_ref, side_ref, total_ref,
):
    blocks, _, lanes = node_ref.shape
    me = lax.axis_index("dom")
    for k in range(blocks):
        total_ref[k] = node_ref[k]
    for o in range(2 * reach):
        present, there = neighbour(me, count, offset_of(o, reach))
        piece = got_ref[there]
        for m in range(width):
            b = send_ref[o, m]
            total_ref[b] = total_ref[b] - jnp.where(present, piece[m : m + 1], 0.0)
    hidden = act_ref.shape[0]
    out_sum = jnp.zeros((hidden, lanes), jnp.float32)
    bias_sum = jnp.zeros((hidden, lanes), jnp.float32)
    grad = jnp.zeros((hidden, f_ref.shape[1]), jnp.float32)
    group = 4
    for c in range(blocks // group):
        highs = []
        lows = []
        for k in range(c * group, (c + 1) * group):
            act = act_ref[:, k * lanes : (k + 1) * lanes]
            node = total_ref[k] * scale
            weighted = act * node
            pre = node - weighted * act
            out_sum = out_sum + weighted
            bias_sum = bias_sum + pre
            high = pre.astype(jnp.bfloat16)
            highs.append(high)
            lows.append((pre - high.astype(jnp.float32)).astype(jnp.bfloat16))
        f = f_ref[c * group * lanes : (c + 1) * group * lanes]
        grad = grad + lax.dot_general(
            jnp.concatenate(highs, axis=1), f, NN, preferred_element_type=jnp.float32
        )
        grad = grad + lax.dot_general(
            jnp.concatenate(lows, axis=1), f, NN, preferred_element_type=jnp.float32
        )
    v = v_ref[...]
    grad_ref[...] = grad * v
    side_ref[:, 0:1] = jnp.sum(bias_sum, axis=1, keepdims=True) * v
    side_ref[:, 1:2] = jnp.sum(out_sum, axis=1, keepdims=True)


def local(
    features, w_input, b_input, w_output, terminal, start_counts, visit_counts, dest_nodes,
    tile_rows, tile_cols, send_blocks, tile_weight,
):
    f32, bf16 = jnp.float32, jnp.bfloat16
    nodes = features.shape[0]
    tiles, lanes, _ = tile_weight.shape
    blocks = nodes // lanes
    rows = terminal.shape[0]
    hidden = w_input.shape[1]
    feat = features.shape[1]
    reach = send_blocks.shape[0] // 2
    width = send_blocks.shape[1]
    slots = 2 * reach * width
    count = lax.axis_size("dom")
    shape = lambda *s: jax.ShapeDtypeStruct(s, f32)
    geometry = (count, reach, width)
    bind = lambda kernel: functools.partial(kernel, *geometry)
    swap = lambda x: lax.all_to_all(x, "dom", 0, 0, tiled=True)
    dest = dest_nodes[:, None]
    column_v = w_output[:, None]

    field = shape(blocks, rows, lanes)
    parcel = shape(count, width * rows, lanes)
    split = pltpu.VMEM((blocks + slots, 2 * rows, lanes), bf16)
    total = pltpu.VMEM((blocks, rows, lanes), f32)
    wide = pltpu.VMEM((blocks + slots, rows, lanes), f32)
    step_flops = 2 * tiles * lanes * lanes * 2 * rows
    step_bytes = tiles * lanes * lanes * 2

    z0, out = call(
        bind(first_kernel), (field, parcel), [], (send_blocks, terminal), 1, nodes * rows, nodes * rows * 8
    )
    far = swap(out)
    act, growth = call(
        network_kernel,
        (shape(hidden, nodes), shape(blocks, 1, lanes)),
        [],
        (w_input.T, b_input[:, None], column_v, features),
        0,
        2 * nodes * hidden * feat,
        nodes * hidden * 4,
    )
    z1, out = call(
        bind(backup_kernel),
        (field, parcel),
        [split, total],
        (tile_rows, tile_cols, send_blocks, tile_weight, z0, far, growth, dest),
        3,
        step_flops,
        step_bytes,
    )
    got = swap(out)
    z2, out = call(
        bind(backup_kernel),
        (field, parcel),
        [split, total],
        (tile_rows, tile_cols, send_blocks, tile_weight, z1, got, growth, dest),
        3,
        step_flops,
        step_bytes,
    )
    got = swap(out)
    values, flow, out = call(
        bind(turn_kernel),
        (shape(rows, nodes), field, parcel),
        [split, total, wide],
        (tile_rows, tile_cols, tile_weight, z2, got, growth, dest, start_counts),
        2,
        2 * step_flops,
        step_bytes,
    )
    got = swap(out)
    first, flow, out = call(
        bind(spread_kernel),
        (field, field, parcel),
        [split, wide],
        (tile_rows, tile_cols, send_blocks, tile_weight, flow, got, growth),
        3,
        step_flops,
        step_bytes,
    )
    got = swap(out)
    node, out = call(
        bind(last_kernel),
        (shape(blocks, 1, lanes), shape(count, 8, lanes)),
        [split, wide, total],
        (
            tile_rows, tile_cols, send_blocks, tile_weight, flow, got, growth,
            z0, z1, z2, first, visit_counts, far,
        ),
        3,
        step_flops,
        step_bytes,
    )
    got = swap(out)
    scale = 1.0 / math.sqrt(nodes * count * rows * lax.axis_size("dest"))
    grad, side = call(
        functools.partial(gradient_kernel, *geometry, scale),
        (shape(hidden, feat), shape(hidden, 2)),
        [pltpu.VMEM((blocks, 1, lanes), f32)],
        (send_blocks, column_v, features, act, node, got),
        1,
        4 * nodes * hidden * feat,
        nodes * hidden * 4,
    )
    every = ("dest", "dom")
    members = count * lax.axis_size("dest")
    packed = jnp.concatenate([grad, side.T.reshape(-1, feat)], axis=0)
    height = packed.shape[0]
    share = -(-height // members)
    share = -(-share // 8) * 8
    packed = jnp.pad(packed, ((0, share * members - height), (0, 0)))
    mine = lax.all_to_all(packed.reshape(members, share, feat), every, 0, 0, tiled=True).sum(axis=0)
    spread = jnp.broadcast_to(mine[None], (members, share, feat))
    summed = lax.all_to_all(spread, every, 0, 0, tiled=True).reshape(members * share, feat)
    side = summed[hidden : hidden + 2 * hidden // feat].reshape(2, hidden)
    return values, summed[:hidden].T, side[0], side[1]


def solution(mesh):
    in_specs = (
        P("dom", None),
        P(),
        P(),
        P(),
        P("dest", "dom"),
        P("dest", "dom"),
        P("dest", "dom"),
        P("dest"),
        P("dom"),
        P("dom"),
        P("dom", None),
        P("dom", None, None),
    )
    out_specs = (P("dest", "dom"), P(), P(), P())
    return jax.shard_map(local, mesh=mesh, in_specs=in_specs, out_specs=out_specs, check_vma=False)
```

```python
import functools
import math

import jax
import jax.numpy as jnp
from jax import lax
from jax.experimental import pallas as pl
from jax.experimental.pallas import tpu as pltpu
from jax.sharding import PartitionSpec as P

STEPS = 3
GOAL_GAIN = 32.0
VMEM_GRANT = 20 << 20

NT = (((1,), (1,)), ((), ()))
NN = (((1,), (0,)), ((), ()))


def offset_of(o, reach):
    return o - reach if o < reach else o - reach + 1


def present(me, count, shift):
    there = me + shift
    return jnp.logical_and(there >= 0, there < count)


def place(me, shift):
    origin = me - shift
    k = jnp.bitwise_xor(origin, me) & 3
    core, side, odd = me & 1, (me >> 1) & 1, (me >> 2) & 1
    apart = (origin >> 2) - (me >> 2)
    here = jnp.where(k == 1, 1 + core, jnp.where(k == 2, 5 - side, 7 - side))
    below = jnp.where(odd == 1, 8, 12) + k
    above = jnp.where(odd == 1, 12, 8) + k
    return jnp.where(apart == 0, here, jnp.where(apart < 0, below, above))


def exchange(odd, even):
    me = lax.axis_index("dom")
    devices = range(lax.axis_size("dom"))
    core_zero = me % 2 == 0
    group_even = (me // 4) % 2 == 0

    def partner(i, flip):
        j = (i // 4 + (1 if (i // 4) % 2 == 1 else -1)) * 4 + i % 4
        return j if j in devices else i ^ 1

    flip = lambda x, bit: lax.ppermute(x, "dom", [(i, i ^ bit) for i in devices])
    near = flip(odd, 1)
    side = flip(
        jnp.stack(
            [
                even[2],
                even[1],
                jnp.where(core_zero, near[2], near[3]),
                jnp.where(core_zero, near[0], near[1]),
            ]
        ),
        2,
    )
    up = jnp.stack([even[3], near[3], side[0], side[2]])
    down = jnp.stack([even[0], near[0], side[1], side[3]])
    first = flip(jnp.where(group_even, up, down), 4)
    second = lax.ppermute(
        jnp.where(group_even, down, up), "dom", [(i, partner(i, 1)) for i in devices]
    )
    return near, side, first, second


def call(kernel, out_shape, scratch, smem, vmem, flops, moved):
    space = lambda kind: pl.BlockSpec(memory_space=kind)
    return pl.pallas_call(
        kernel,
        out_shape=out_shape,
        in_specs=[space(pltpu.SMEM)] * len(smem) + [space(pltpu.VMEM)] * len(vmem),
        out_specs=jax.tree.map(lambda _: space(pltpu.VMEM), out_shape),
        scratch_shapes=scratch,
        compiler_params=pltpu.CompilerParams(vmem_limit_bytes=VMEM_GRANT),
        cost_estimate=pl.CostEstimate(flops=flops, bytes_accessed=moved, transcendentals=0),
    )(*smem, *vmem)


def store_split(ref, k, x):
    rows = x.shape[0]
    high = x.astype(jnp.bfloat16)
    low = (x - high.astype(jnp.float32)).astype(jnp.bfloat16)
    ref[k, :rows] = high
    ref[k, rows:] = low


def product(lhs, rhs, dims):
    both = lax.dot_general(lhs, rhs, dims, preferred_element_type=jnp.float32)
    rows = both.shape[0] // 2
    return both[:rows] + both[rows:]


def offsets(reach):
    return [offset_of(o, reach) for o in range(2 * reach)]


def send_items(odd_ref, even_ref, reach, width, sign, item):
    ways = offsets(reach)
    odds = [f for f in ways if f % 2]
    evens = [f for f in ways if f % 2 == 0]
    for o, f in enumerate(ways):
        shift = sign * f
        ref, at = (odd_ref, odds.index(shift)) if shift % 2 else (even_ref, evens.index(shift))
        for m in range(width):
            piece = item(o, m)
            rows = piece.shape[0]
            ref[at, m * rows : (m + 1) * rows] = piece


def collect(all_ref, parts):
    at = 0
    for part in parts:
        for k in range(part.shape[0]):
            all_ref[at] = part[k]
            at += 1


def network_kernel(w_ref, b_ref, v_ref, f_ref, act_ref, growth_ref):
    lanes = growth_ref.shape[2]
    hidden = act_ref.shape[0]
    group = 2
    w = w_ref[...].T
    b = jnp.broadcast_to(b_ref[...], (lanes, hidden)).T
    v = jnp.broadcast_to(v_ref[...], (lanes, hidden)).T
    for c in range(growth_ref.shape[0] // group):
        f = f_ref[c * group * lanes : (c + 1) * group * lanes]
        pre = lax.dot_general(w, f, NT, preferred_element_type=jnp.float32)
        for k in range(group):
            at = c * group + k
            act = jnp.tanh(pre[:, k * lanes : (k + 1) * lanes] + b)
            act_ref[:, at * lanes : (at + 1) * lanes] = act
            growth_ref[at] = jnp.exp(jnp.sum(act * v, axis=0, keepdims=True))


def first_kernel(reach, width, send_ref, term_ref, z_ref, split_ref, odd_ref, even_ref):
    blocks, _, lanes = z_ref.shape
    for k in range(blocks):
        z = jnp.exp(term_ref[:, k * lanes : (k + 1) * lanes])
        z_ref[k] = z
        store_split(split_ref, k, z)
    send_items(odd_ref, even_ref, reach, width, 1, lambda o, m: z_ref[send_ref[o, m]])


def diagonal_kernel(w_ref, split_ref, sum_ref):
    for k in range(split_ref.shape[0]):
        sum_ref[k] = product(split_ref[k], w_ref[k], NT)


def back_diagonal_kernel(w_ref, split_ref, part_ref, sum_ref):
    for k in range(split_ref.shape[0]):
        sum_ref[k] = part_ref[k] + product(split_ref[k], w_ref[k], NN)


def backed_up(
    reach, width, rows_ref, cols_ref, w_ref, split_ref, part_ref, parts, all_ref, ext_ref, sum_ref
):
    blocks, rows, _ = part_ref.shape
    me = lax.axis_index("dom")
    collect(all_ref, parts)
    for o, f in enumerate(offsets(reach)):
        at = place(me, f)
        for m in range(width):
            store_split(
                ext_ref, blocks + o * width + m, all_ref[at, m * rows : (m + 1) * rows]
            )
    for k in range(blocks):
        ext_ref[k] = split_ref[k]
        sum_ref[k] = part_ref[k]
    for t in range(blocks, w_ref.shape[0]):
        r = rows_ref[t]
        sum_ref[r] = sum_ref[r] + product(ext_ref[cols_ref[t]], w_ref[t], NT)


def goal_of(dest_ref, rows, lanes):
    row = lax.broadcasted_iota(jnp.int32, (rows, lanes), 0)
    dest = jnp.zeros((rows, lanes), jnp.int32)
    for d in range(rows):
        dest = jnp.where(row == d, dest_ref[d], dest)
    return dest


def with_goal(k, growth_ref, sum_ref, dest, me):
    blocks, rows, lanes = sum_ref.shape
    node = (me * blocks + k) * lanes + lax.broadcasted_iota(jnp.int32, (rows, lanes), 1)
    return growth_ref[k] * sum_ref[k] + jnp.where(node == dest, GOAL_GAIN, 0.0)


def backup_kernel(
    reach, width, rows_ref, cols_ref, send_ref, dest_ref, w_ref, split_ref, part_ref, growth_ref,
    near_ref, side_ref, first_ref, second_ref,
    z_ref, next_ref, odd_ref, even_ref, all_ref, ext_ref, sum_ref,
):
    blocks, rows, lanes = z_ref.shape
    me = lax.axis_index("dom")
    backed_up(
        reach, width, rows_ref, cols_ref, w_ref, split_ref, part_ref,
        (near_ref, side_ref, first_ref, second_ref), all_ref, ext_ref, sum_ref,
    )
    dest = goal_of(dest_ref, rows, lanes)
    for k in range(blocks):
        z = with_goal(k, growth_ref, sum_ref, dest, me)
        z_ref[k] = z
        store_split(next_ref, k, z)
    send_items(odd_ref, even_ref, reach, width, 1, lambda o, m: z_ref[send_ref[o, m]])


def spread_out(rows_ref, cols_ref, w_ref, split_ref, ext_ref, blocks):
    for k in range(ext_ref.shape[0]):
        ext_ref[k] = jnp.zeros(ext_ref.shape[1:], jnp.float32)
    for t in range(blocks, w_ref.shape[0]):
        c = cols_ref[t]
        ext_ref[c] = ext_ref[c] + product(split_ref[rows_ref[t]], w_ref[t], NN)


def turn_kernel(
    reach, width, rows_ref, cols_ref, dest_ref, w_ref, split_ref, part_ref, growth_ref,
    near_ref, side_ref, first_ref, second_ref, start_ref,
    values_ref, next_ref, rest_ref, odd_ref, even_ref, all_ref, ext_ref, sum_ref, flow_ref,
):
    blocks, rows, lanes = part_ref.shape
    me = lax.axis_index("dom")
    backed_up(
        reach, width, rows_ref, cols_ref, w_ref, split_ref, part_ref,
        (near_ref, side_ref, first_ref, second_ref), all_ref, ext_ref, sum_ref,
    )
    dest = goal_of(dest_ref, rows, lanes)
    for k in range(blocks):
        z = with_goal(k, growth_ref, sum_ref, dest, me)
        span = slice(k * lanes, (k + 1) * lanes)
        values_ref[:, span] = jnp.log(z)
        store_split(next_ref, k, growth_ref[k] * start_ref[:, span].astype(jnp.float32) / z)
    spread_out(rows_ref, cols_ref, w_ref, next_ref, flow_ref, blocks)
    for k in range(blocks):
        rest_ref[k] = flow_ref[k]
    send_items(
        odd_ref, even_ref, reach, width, -1, lambda o, m: flow_ref[blocks + o * width + m]
    )


def take_returned(count, reach, width, send_ref, parts, all_ref, into_ref):
    rows = into_ref.shape[1]
    me = lax.axis_index("dom")
    collect(all_ref, parts)
    for o, f in enumerate(offsets(reach)):
        there = present(me, count, f)
        at = place(me, -f)
        for m in range(width):
            b = send_ref[o, m]
            piece = all_ref[at, m * rows : (m + 1) * rows]
            into_ref[b] = into_ref[b] + jnp.where(there, piece, 0.0)


def flows(
    count, reach, width, rows_ref, cols_ref, send_ref, w_ref, growth_ref, sum_ref, parts,
    u_ref, next_ref, rest_ref, all_ref, flow_ref,
):
    blocks = u_ref.shape[0]
    for k in range(blocks):
        u_ref[k] = sum_ref[k]
    take_returned(count, reach, width, send_ref, parts, all_ref, u_ref)
    for k in range(blocks):
        store_split(next_ref, k, growth_ref[k] * u_ref[k])
    spread_out(rows_ref, cols_ref, w_ref, next_ref, flow_ref, blocks)
    for k in range(blocks):
        rest_ref[k] = flow_ref[k]


def spread_kernel(
    count, reach, width, rows_ref, cols_ref, send_ref, w_ref, growth_ref, sum_ref,
    near_ref, side_ref, first_ref, second_ref,
    u_ref, next_ref, rest_ref, odd_ref, even_ref, all_ref, flow_ref,
):
    blocks = u_ref.shape[0]
    flows(
        count, reach, width, rows_ref, cols_ref, send_ref, w_ref, growth_ref, sum_ref,
        (near_ref, side_ref, first_ref, second_ref), u_ref, next_ref, rest_ref, all_ref, flow_ref,
    )
    send_items(
        odd_ref, even_ref, reach, width, -1, lambda o, m: flow_ref[blocks + o * width + m]
    )


def last_kernel(
    count, reach, width, rows_ref, cols_ref, send_ref, w_ref, growth_ref, sum_ref,
    near_ref, side_ref, first_ref, second_ref, z_near_ref, z_side_ref, z_first_ref, z_second_ref,
    u_ref, next_ref, rest_ref, odd_ref, even_ref, all_ref, flow_ref, far_ref,
):
    blocks, rows, lanes = u_ref.shape
    me = lax.axis_index("dom")
    flows(
        count, reach, width, rows_ref, cols_ref, send_ref, w_ref, growth_ref, sum_ref,
        (near_ref, side_ref, first_ref, second_ref), u_ref, next_ref, rest_ref, all_ref, flow_ref,
    )
    collect(far_ref, (z_near_ref, z_side_ref, z_first_ref, z_second_ref))
    ways = offsets(reach)
    odds = [f for f in ways if f % 2]
    evens = [f for f in ways if f % 2 == 0]
    row = lax.broadcasted_iota(jnp.int32, odd_ref.shape[1:], 0)
    for o, f in enumerate(ways):
        at = place(me, f)
        item = jnp.zeros(odd_ref.shape[1:], jnp.float32)
        for m in range(width):
            lost = far_ref[at, m * rows : (m + 1) * rows] * flow_ref[blocks + o * width + m]
            item = jnp.where(row == m, jnp.sum(lost, axis=0, keepdims=True), item)
        if f % 2:
            odd_ref[odds.index(-f)] = item
        else:
            even_ref[evens.index(-f)] = item


def node_kernel(
    w_ref, split_ref, part_ref, z0_ref, z1_ref, z2_ref, u1_ref, u2_ref, visit_ref, node_ref
):
    blocks, _, lanes = part_ref.shape
    for k in range(blocks):
        u3 = part_ref[k] + product(split_ref[k], w_ref[k], NN)
        left = (
            visit_ref[:, k * lanes : (k + 1) * lanes].astype(jnp.float32)
            - z2_ref[k] * u1_ref[k]
            - z1_ref[k] * u2_ref[k]
            - z0_ref[k] * u3
        )
        node_ref[k] = jnp.sum(left, axis=0, keepdims=True)


def gradient_kernel(
    count, reach, width, scale, send_ref, v_ref, f_ref, act_ref, node_ref,
    near_ref, side_ref, first_ref, second_ref, grad_ref, total_ref, all_ref,
):
    blocks, _, lanes = node_ref.shape
    me = lax.axis_index("dom")
    collect(all_ref, (near_ref, side_ref, first_ref, second_ref))
    for k in range(blocks):
        total_ref[k] = node_ref[k]
    for o, f in enumerate(offsets(reach)):
        there = present(me, count, f)
        at = place(me, -f)
        for m in range(width):
            b = send_ref[o, m]
            total_ref[b] = total_ref[b] - jnp.where(there, all_ref[at, m : m + 1], 0.0)
    hidden = act_ref.shape[0]
    out_sum = jnp.zeros((hidden, lanes), jnp.float32)
    bias_sum = jnp.zeros((hidden, lanes), jnp.float32)
    grad = jnp.zeros((hidden, f_ref.shape[1]), jnp.float32)
    group = 4
    for c in range(blocks // group):
        highs = []
        lows = []
        for k in range(c * group, (c + 1) * group):
            act = act_ref[:, k * lanes : (k + 1) * lanes]
            node = total_ref[k] * scale
            weighted = act * node
            pre = node - weighted * act
            out_sum = out_sum + weighted
            bias_sum = bias_sum + pre
            high = pre.astype(jnp.bfloat16)
            highs.append(high)
            lows.append((pre - high.astype(jnp.float32)).astype(jnp.bfloat16))
        f = f_ref[c * group * lanes : (c + 1) * group * lanes]
        grad = grad + lax.dot_general(
            jnp.concatenate(highs, axis=1), f, NN, preferred_element_type=jnp.float32
        )
        grad = grad + lax.dot_general(
            jnp.concatenate(lows, axis=1), f, NN, preferred_element_type=jnp.float32
        )
    v = v_ref[...]
    parts = hidden // lanes
    for j in range(parts):
        span = slice(j * lanes, (j + 1) * lanes)
        turned = grad[span].T * v[:, span]
        for i in range(f_ref.shape[1] // 8):
            at = (i * parts + j) * 8
            grad_ref[at : at + 8] = turned[i * 8 : (i + 1) * 8]
    ones = jnp.ones((8, lanes), jnp.float32)
    across = lambda x: lax.dot_general(
        ones, x, NT, precision=lax.Precision.HIGHEST, preferred_element_type=jnp.float32
    )[:1]
    bias = across(bias_sum) * v
    out = across(out_sum)
    at = hidden * f_ref.shape[1] // lanes
    for j in range(parts):
        span = slice(j * lanes, (j + 1) * lanes)
        grad_ref[at + j : at + j + 1] = bias[:, span]
        grad_ref[at + parts + j : at + parts + j + 1] = out[:, span]
    grad_ref[at + 2 * parts :] = jnp.zeros_like(grad_ref[at + 2 * parts :])


def local(
    features, w_input, b_input, w_output, terminal, start_counts, visit_counts, dest_nodes,
    tile_rows, tile_cols, send_blocks, tile_weight,
):
    f32, bf16 = jnp.float32, jnp.bfloat16
    nodes, feat = features.shape
    tiles, lanes, _ = tile_weight.shape
    blocks = nodes // lanes
    rows = terminal.shape[0]
    hidden = w_input.shape[1]
    reach = send_blocks.shape[0] // 2
    width = send_blocks.shape[1]
    slots = 2 * reach * width
    count = lax.axis_size("dom")
    assert reach == 4 and count % 8 == 0
    shape = lambda *s: jax.ShapeDtypeStruct(s, f32)
    row_v = w_output[None, :]

    field = shape(blocks, rows, lanes)
    halves = jax.ShapeDtypeStruct((blocks, 2 * rows, lanes), bf16)
    parcel = shape(reach, width * rows, lanes)
    small = shape(reach, 8, lanes)
    all_s = pltpu.VMEM((4 * reach, width * rows, lanes), f32)
    ext_s = pltpu.VMEM((blocks + slots, 2 * rows, lanes), bf16)
    sum_s = pltpu.VMEM((blocks, rows, lanes), f32)
    flow_s = pltpu.VMEM((blocks + slots, rows, lanes), f32)
    bind = lambda kernel, *lead: functools.partial(kernel, *lead, reach, width)
    flops = 2 * tiles * lanes * lanes * 2 * rows
    moved = tiles * lanes * lanes * 2

    def diagonal(split):
        return call(diagonal_kernel, field, [], (), (tile_weight, split), flops, moved)

    def back_diagonal(split, rest):
        return call(back_diagonal_kernel, field, [], (), (tile_weight, split, rest), flops, moved)

    z0, split, odd, even = call(
        bind(first_kernel), (field, halves, parcel, parcel), [], (send_blocks,), (terminal,), flops, moved
    )
    far = exchange(odd, even)
    act, growth = call(
        network_kernel,
        (shape(hidden, nodes), shape(blocks, 1, lanes)),
        [],
        (),
        (w_input, b_input[None, :], row_v, features),
        2 * nodes * hidden * feat,
        nodes * hidden * 4,
    )

    def backup(split, got):
        return call(
            bind(backup_kernel),
            (field, halves, parcel, parcel),
            [all_s, ext_s, sum_s],
            (tile_rows, tile_cols, send_blocks, dest_nodes),
            (tile_weight, split, diagonal(split), growth, *got),
            flops,
            moved,
        )

    z1, split, odd, even = backup(split, far)
    z2, split, odd, even = backup(split, exchange(odd, even))
    got = exchange(odd, even)
    values, split, rest, odd, even = call(
        bind(turn_kernel),
        (shape(rows, nodes), halves, field, parcel, parcel),
        [all_s, ext_s, sum_s, flow_s],
        (tile_rows, tile_cols, dest_nodes),
        (tile_weight, split, diagonal(split), growth, *got, start_counts),
        2 * flops,
        moved,
    )
    got = exchange(odd, even)
    u1, split, rest, odd, even = call(
        bind(spread_kernel, count),
        (field, halves, field, parcel, parcel),
        [all_s, flow_s],
        (tile_rows, tile_cols, send_blocks),
        (tile_weight, growth, back_diagonal(split, rest), *got),
        flops,
        moved,
    )
    got = exchange(odd, even)
    u2, split, rest, odd, even = call(
        bind(last_kernel, count),
        (field, halves, field, small, small),
        [all_s, flow_s, all_s],
        (tile_rows, tile_cols, send_blocks),
        (tile_weight, growth, back_diagonal(split, rest), *got, *far),
        flops,
        moved,
    )
    got = exchange(odd, even)
    node = call(
        node_kernel,
        shape(blocks, 1, lanes),
        [],
        (),
        (tile_weight, split, rest, z0, z1, z2, u1, u2, visit_counts),
        flops,
        moved,
    )
    every = ("dest", "dom")
    members = count * lax.axis_size("dest")
    used = hidden * feat // lanes + 2 * hidden // lanes
    share = -(-used // members)
    scale = 1.0 / math.sqrt(nodes * count * rows * lax.axis_size("dest"))
    packed = call(
        functools.partial(gradient_kernel, count, reach, width, scale),
        shape(share * members, lanes),
        [pltpu.VMEM((blocks, 1, lanes), f32), pltpu.VMEM((4 * reach, 8, lanes), f32)],
        (send_blocks,),
        (row_v, features, act, node, *got),
        4 * nodes * hidden * feat,
        nodes * hidden * 4,
    )
    packed = packed.reshape(members, 1, share * lanes)
    mine = lax.all_to_all(packed, every, 0, 0, tiled=True).sum(axis=0, keepdims=True)
    spread = jnp.broadcast_to(mine, packed.shape)
    summed = lax.all_to_all(spread, every, 0, 0, tiled=True).reshape(share * members, lanes)
    side = summed[hidden * feat // lanes : used].reshape(2, hidden)
    grad = summed[: hidden * feat // lanes].reshape(feat // 8, hidden // lanes, 8, lanes)
    return values, grad.transpose(0, 2, 1, 3).reshape(feat, hidden), side[0], side[1]


def solution(mesh):
    in_specs = (
        P("dom", None),
        P(),
        P(),
        P(),
        P("dest", "dom"),
        P("dest", "dom"),
        P("dest", "dom"),
        P("dest"),
        P("dom"),
        P("dom"),
        P("dom", None),
        P("dom", None, None),
    )
    out_specs = (P("dest", "dom"), P(), P(), P())
    return jax.shard_map(local, mesh=mesh, in_specs=in_specs, out_specs=out_specs, check_vma=False)
```

```python
import functools
import math

import jax
import jax.numpy as jnp
from jax import lax
from jax.experimental import pallas as pl
from jax.experimental.pallas import tpu as pltpu
from jax.sharding import PartitionSpec as P

STEPS = 3
GOAL_GAIN = 32.0
VMEM_GRANT = 20 << 20

HOLD = lambda x: pltpu.with_memory_space_constraint(x, pltpu.HBM)
NT = (((1,), (1,)), ((), ()))
NN = (((1,), (0,)), ((), ()))


def offset_of(o, reach):
    return o - reach if o < reach else o - reach + 1


def present(me, count, shift):
    there = me + shift
    return jnp.logical_and(there >= 0, there < count)


def place(me, shift):
    origin = me - shift
    k = jnp.bitwise_xor(origin, me) & 3
    core, side, odd = me & 1, (me >> 1) & 1, (me >> 2) & 1
    apart = (origin >> 2) - (me >> 2)
    here = jnp.where(k == 1, 1 + core, jnp.where(k == 2, 5 - side, 7 - side))
    below = jnp.where(odd == 1, 8, 12) + k
    above = jnp.where(odd == 1, 12, 8) + k
    return jnp.where(apart == 0, here, jnp.where(apart < 0, below, above))


def exchange(odd, even, work=None):
    me = lax.axis_index("dom")
    devices = range(lax.axis_size("dom"))
    core_zero = me % 2 == 0
    group_even = (me // 4) % 2 == 0

    def partner(i, flip):
        j = (i // 4 + (1 if (i // 4) % 2 == 1 else -1)) * 4 + i % 4
        return j if j in devices else i ^ 1

    flip = lambda x, bit: lax.ppermute(x, "dom", [(i, i ^ bit) for i in devices])
    near = flip(odd, 1)
    side = flip(
        jnp.stack(
            [
                even[2],
                even[1],
                jnp.where(core_zero, near[2], near[3]),
                jnp.where(core_zero, near[0], near[1]),
            ]
        ),
        2,
    )
    done = None
    if work is not None:
        side, done = lax.optimization_barrier((side, work(near)))
    up = jnp.stack([even[3], near[3], side[0], side[2]])
    down = jnp.stack([even[0], near[0], side[1], side[3]])
    first = flip(jnp.where(group_even, up, down), 4)
    second = lax.ppermute(
        jnp.where(group_even, down, up), "dom", [(i, partner(i, 1)) for i in devices]
    )
    return (near, side, first, second), done


def call(kernel, out_shape, scratch, smem, vmem, flops, moved, hbm=(), smem_out=False, after=()):
    space = lambda kind: pl.BlockSpec(memory_space=kind)
    out_specs = jax.tree.map(lambda _: space(pltpu.VMEM), out_shape)
    if smem_out:
        out_specs = (space(pltpu.SMEM), *out_specs[1:])
    if after:
        inner, lead, span = kernel, len(hbm) + len(smem) + len(vmem), len(after)
        kernel = lambda *refs: inner(*refs[:lead], *refs[lead + span :])
    hbm = [HOLD(x) for x in hbm]
    return pl.pallas_call(
        kernel,
        out_shape=out_shape,
        in_specs=[space(pltpu.HBM)] * len(hbm)
        + [space(pltpu.SMEM)] * len(smem)
        + [space(pltpu.VMEM)] * len(vmem)
        + [space(pl.ANY)] * len(after),
        out_specs=out_specs,
        scratch_shapes=scratch,
        compiler_params=pltpu.CompilerParams(vmem_limit_bytes=VMEM_GRANT),
        cost_estimate=pl.CostEstimate(flops=flops, bytes_accessed=moved, transcendentals=0),
    )(*hbm, *smem, *vmem, *after)


def store_split(ref, k, x):
    rows = x.shape[0]
    high = x.astype(jnp.bfloat16)
    low = (x - high.astype(jnp.float32)).astype(jnp.bfloat16)
    ref[k, :rows] = high
    ref[k, rows:] = low


def product(lhs, rhs, dims):
    both = lax.dot_general(lhs, rhs, dims, preferred_element_type=jnp.float32)
    rows = both.shape[0] // 2
    return both[:rows] + both[rows:]


def offsets(reach):
    return [offset_of(o, reach) for o in range(2 * reach)]


def send_items(odd_ref, even_ref, reach, width, sign, item):
    ways = offsets(reach)
    odds = [f for f in ways if f % 2]
    evens = [f for f in ways if f % 2 == 0]
    for o, f in enumerate(ways):
        shift = sign * f
        ref, at = (odd_ref, odds.index(shift)) if shift % 2 else (even_ref, evens.index(shift))
        for m in range(width):
            piece = item(o, m)
            rows = piece.shape[0]
            ref[at, m * rows : (m + 1) * rows] = piece


def collect(all_ref, parts):
    at = 0
    for part in parts:
        for k in range(part.shape[0]):
            all_ref[at] = part[k]
            at += 1


class Plan:
    def __init__(self, blocks, tiles, slots, rows):
        at = 0
        for name, size in (
            ("far_t", slots), ("far_r", slots), ("far_c", slots),
            ("near_t", tiles - blocks), ("near_r", tiles - blocks), ("near_c", tiles - blocks),
            ("send", slots), ("dest", rows), ("near", 1), ("far", 1),
        ):
            setattr(self, name, at)
            at += size
        self.size = at
        self.blocks, self.slots, self.extra = blocks, slots, tiles - blocks


def load_kernel(
    plan, rows_hbm, cols_hbm, send_hbm, dest_hbm, tile_hbm, f_hbm, w_hbm, b_hbm, v_hbm,
    plan_ref, tile_ref, f_ref, w_ref, b_ref, v_ref, rows_ref, cols_ref, send_ref, dest_ref, sem, small,
):
    smalls = [
        pltpu.make_async_copy(src, dst, small.at[k])
        for k, (src, dst) in enumerate(
            ((rows_hbm, rows_ref), (cols_hbm, cols_ref), (send_hbm, send_ref), (dest_hbm, dest_ref))
        )
    ]
    larges = [
        pltpu.make_async_copy(src, dst, sem.at[k])
        for k, (src, dst) in enumerate(
            ((f_hbm, f_ref), (w_hbm, w_ref), (b_hbm, b_ref), (v_hbm, v_ref), (tile_hbm, tile_ref))
        )
    ]
    for copy in smalls + larges:
        copy.start()
    for copy in smalls:
        copy.wait()
    for k in range(plan.size):
        plan_ref[k] = 0
    width = send_ref.shape[0]
    for k in range(plan.slots):
        plan_ref[plan.far_c + k] = plan.blocks
        plan_ref[plan.send + k] = send_ref[k % width, k // width]
    for k in range(dest_ref.shape[0]):
        plan_ref[plan.dest + k] = dest_ref[k]

    def sort_tile(k, counts):
        near, far = counts
        t = plan.blocks + k
        r, c = rows_ref[t], cols_ref[t]
        apart = c >= plan.blocks
        at = jnp.where(apart, plan.far_t + far, plan.near_t + near)
        step = jnp.where(apart, plan.slots, plan.extra)
        plan_ref[at] = t
        plan_ref[at + step] = r
        plan_ref[at + 2 * step] = c
        one = apart.astype(jnp.int32)
        return near + 1 - one, far + one

    near, far = lax.fori_loop(0, plan.extra, sort_tile, (jnp.int32(0), jnp.int32(0)))
    plan_ref[plan.near] = near
    plan_ref[plan.far] = far
    for copy in larges:
        copy.wait()


def network_kernel(w_ref, b_ref, v_ref, f_ref, act_ref, growth_ref):
    lanes = growth_ref.shape[2]
    hidden = act_ref.shape[0]
    group = 2
    w = w_ref[...].T
    b = jnp.broadcast_to(b_ref[...], (lanes, hidden)).T
    v = jnp.broadcast_to(v_ref[...], (lanes, hidden)).T
    for c in range(growth_ref.shape[0] // group):
        f = f_ref[c * group * lanes : (c + 1) * group * lanes]
        pre = lax.dot_general(w, f, NT, preferred_element_type=jnp.float32)
        for k in range(group):
            at = c * group + k
            act = jnp.tanh(pre[:, k * lanes : (k + 1) * lanes] + b)
            act_ref[:, at * lanes : (at + 1) * lanes] = act
            growth_ref[at] = jnp.exp(jnp.sum(act * v, axis=0, keepdims=True))


def first_kernel(
    reach, width, send_hbm, term_hbm, z_ref, split_ref, odd_ref, even_ref, send_ref, term_ref, sem, small
):
    blocks, _, lanes = z_ref.shape
    parts = sem.shape[0]
    span = blocks // parts
    asked = pltpu.make_async_copy(send_hbm, send_ref, small)
    cut = lambda ref, i: ref.at[:, i * span * lanes : (i + 1) * span * lanes]
    copies = [
        pltpu.make_async_copy(cut(term_hbm, i), cut(term_ref, i), sem.at[i]) for i in range(parts)
    ]
    asked.start()
    for copy in copies:
        copy.start()
    for i, copy in enumerate(copies):
        copy.wait()
        for k in range(i * span, (i + 1) * span):
            z = jnp.exp(term_ref[:, k * lanes : (k + 1) * lanes])
            z_ref[k] = z
            store_split(split_ref, k, z)
    asked.wait()
    send_items(odd_ref, even_ref, reach, width, 1, lambda o, m: z_ref[send_ref[m, o]])


def near_products(plan, plan_ref, w_ref, split_ref, sum_ref, forward):
    dims = NT if forward else NN
    for k in range(plan.blocks):
        sum_ref[k] = product(split_ref[k], w_ref[k], dims)
    count = plan_ref[plan.near]
    for k in range(plan.extra):
        r, c = plan_ref[plan.near_r + k], plan_ref[plan.near_c + k]
        source, into = (c, r) if forward else (r, c)
        into = jnp.where(k < count, into, plan.blocks)
        sum_ref[into] = sum_ref[into] + product(
            split_ref[source], w_ref[plan_ref[plan.near_t + k]], dims
        )


def near_kernel(plan, forward, plan_ref, w_ref, split_ref, sum_ref):
    near_products(plan, plan_ref, w_ref, split_ref, sum_ref, forward)


def backed_up(
    plan, reach, width, plan_ref, w_ref, part_ref, parts, all_ref, ext_ref, sum_ref
):
    rows = part_ref.shape[1]
    me = lax.axis_index("dom")
    collect(all_ref, parts)
    for o, f in enumerate(offsets(reach)):
        at = place(me, f)
        for m in range(width):
            store_split(ext_ref, o * width + m, all_ref[at, m * rows : (m + 1) * rows])
    for k in range(plan.blocks):
        sum_ref[k] = part_ref[k]
    count = plan_ref[plan.far]
    for k in range(plan.slots):
        slot = plan_ref[plan.far_c + k] - plan.blocks
        into = jnp.where(k < count, plan_ref[plan.far_r + k], plan.blocks)
        sum_ref[into] = sum_ref[into] + product(
            ext_ref[slot], w_ref[plan_ref[plan.far_t + k]], NT
        )


def goal_of(plan, plan_ref, rows, lanes):
    row = lax.broadcasted_iota(jnp.int32, (rows, lanes), 0)
    dest = jnp.zeros((rows, lanes), jnp.int32)
    for d in range(rows):
        dest = jnp.where(row == d, plan_ref[plan.dest + d], dest)
    return dest


def with_goal(k, blocks, growth_ref, sum_ref, dest, me):
    _, rows, lanes = sum_ref.shape
    node = (me * blocks + k) * lanes + lax.broadcasted_iota(jnp.int32, (rows, lanes), 1)
    return growth_ref[k] * sum_ref[k] + jnp.where(node == dest, GOAL_GAIN, 0.0)


def backup_kernel(
    plan, reach, width, plan_ref, w_ref, part_ref, growth_ref,
    near_ref, side_ref, first_ref, second_ref,
    z_ref, next_ref, odd_ref, even_ref, all_ref, ext_ref, sum_ref,
):
    blocks, rows, lanes = z_ref.shape
    me = lax.axis_index("dom")
    backed_up(
        plan, reach, width, plan_ref, w_ref, part_ref,
        (near_ref, side_ref, first_ref, second_ref), all_ref, ext_ref, sum_ref,
    )
    dest = goal_of(plan, plan_ref, rows, lanes)
    for k in range(blocks):
        z = with_goal(k, blocks, growth_ref, sum_ref, dest, me)
        z_ref[k] = z
        store_split(next_ref, k, z)
    send_items(
        odd_ref, even_ref, reach, width, 1,
        lambda o, m: z_ref[plan_ref[plan.send + o * width + m]],
    )


def far_flows(plan, plan_ref, w_ref, split_ref, flow_ref):
    for k in range(plan.slots + 1):
        flow_ref[k] = jnp.zeros(flow_ref.shape[1:], jnp.float32)
    count = plan_ref[plan.far]
    for k in range(plan.slots):
        slot = plan_ref[plan.far_c + k] - plan.blocks
        into = jnp.where(k < count, slot, plan.slots)
        flow_ref[into] = flow_ref[into] + product(
            split_ref[plan_ref[plan.far_r + k]], w_ref[plan_ref[plan.far_t + k]], NN
        )


def turn_kernel(
    plan, reach, width, plan_ref, w_ref, part_ref, growth_ref,
    near_ref, side_ref, first_ref, second_ref, start_ref,
    values_ref, next_ref, odd_ref, even_ref, all_ref, ext_ref, sum_ref, flow_ref,
):
    blocks = plan.blocks
    _, rows, lanes = part_ref.shape
    me = lax.axis_index("dom")
    backed_up(
        plan, reach, width, plan_ref, w_ref, part_ref,
        (near_ref, side_ref, first_ref, second_ref), all_ref, ext_ref, sum_ref,
    )
    dest = goal_of(plan, plan_ref, rows, lanes)
    for k in range(blocks):
        z = with_goal(k, blocks, growth_ref, sum_ref, dest, me)
        span = slice(k * lanes, (k + 1) * lanes)
        values_ref[:, span] = jnp.log(z)
        store_split(next_ref, k, growth_ref[k] * start_ref[:, span].astype(jnp.float32) / z)
    far_flows(plan, plan_ref, w_ref, next_ref, flow_ref)
    send_items(odd_ref, even_ref, reach, width, -1, lambda o, m: flow_ref[o * width + m])


def flows(
    plan, count, reach, width, plan_ref, w_ref, growth_ref, sum_ref, parts,
    u_ref, next_ref, all_ref, flow_ref,
):
    blocks, rows, _ = u_ref.shape
    me = lax.axis_index("dom")
    for k in range(blocks):
        u_ref[k] = sum_ref[k]
    collect(all_ref, parts)
    for o, f in enumerate(offsets(reach)):
        there = present(me, count, f)
        at = place(me, -f)
        for m in range(width):
            b = plan_ref[plan.send + o * width + m]
            piece = all_ref[at, m * rows : (m + 1) * rows]
            u_ref[b] = u_ref[b] + jnp.where(there, piece, 0.0)
    for k in range(blocks):
        store_split(next_ref, k, growth_ref[k] * u_ref[k])
    far_flows(plan, plan_ref, w_ref, next_ref, flow_ref)


def spread_kernel(
    plan, count, reach, width, plan_ref, w_ref, growth_ref, sum_ref,
    near_ref, side_ref, first_ref, second_ref,
    u_ref, next_ref, odd_ref, even_ref, all_ref, flow_ref,
):
    flows(
        plan, count, reach, width, plan_ref, w_ref, growth_ref, sum_ref,
        (near_ref, side_ref, first_ref, second_ref), u_ref, next_ref, all_ref, flow_ref,
    )
    send_items(odd_ref, even_ref, reach, width, -1, lambda o, m: flow_ref[o * width + m])


def last_kernel(
    plan, count, reach, width, plan_ref, w_ref, growth_ref, sum_ref,
    near_ref, side_ref, first_ref, second_ref, z_near_ref, z_side_ref, z_first_ref, z_second_ref,
    u_ref, next_ref, odd_ref, even_ref, all_ref, flow_ref, far_ref,
):
    rows = u_ref.shape[1]
    me = lax.axis_index("dom")
    flows(
        plan, count, reach, width, plan_ref, w_ref, growth_ref, sum_ref,
        (near_ref, side_ref, first_ref, second_ref), u_ref, next_ref, all_ref, flow_ref,
    )
    collect(far_ref, (z_near_ref, z_side_ref, z_first_ref, z_second_ref))
    ways = offsets(reach)
    odds = [f for f in ways if f % 2]
    evens = [f for f in ways if f % 2 == 0]
    row = lax.broadcasted_iota(jnp.int32, odd_ref.shape[1:], 0)
    for o, f in enumerate(ways):
        at = place(me, f)
        item = jnp.zeros(odd_ref.shape[1:], jnp.float32)
        for m in range(width):
            lost = far_ref[at, m * rows : (m + 1) * rows] * flow_ref[o * width + m]
            item = jnp.where(row == m, jnp.sum(lost, axis=0, keepdims=True), item)
        if f % 2:
            odd_ref[odds.index(-f)] = item
        else:
            even_ref[evens.index(-f)] = item


def node_kernel(
    plan, plan_ref, w_ref, split_ref, z0_ref, z1_ref, z2_ref, u1_ref, u2_ref, visit_ref,
    node_ref, sum_ref,
):
    blocks, _, lanes = z0_ref.shape
    near_products(plan, plan_ref, w_ref, split_ref, sum_ref, False)
    for k in range(blocks):
        left = (
            visit_ref[:, k * lanes : (k + 1) * lanes].astype(jnp.float32)
            - z2_ref[k] * u1_ref[k]
            - z1_ref[k] * u2_ref[k]
            - z0_ref[k] * sum_ref[k]
        )
        node_ref[k] = jnp.sum(left, axis=0, keepdims=True)


def gradient_kernel(
    plan, count, reach, width, scale, plan_ref, v_ref, f_ref, act_ref, node_ref,
    near_ref, side_ref, first_ref, second_ref, grad_ref, total_ref, all_ref,
):
    blocks, _, lanes = node_ref.shape
    me = lax.axis_index("dom")
    collect(all_ref, (near_ref, side_ref, first_ref, second_ref))
    for k in range(blocks):
        total_ref[k] = node_ref[k]
    for o, f in enumerate(offsets(reach)):
        there = present(me, count, f)
        at = place(me, -f)
        for m in range(width):
            b = plan_ref[plan.send + o * width + m]
            total_ref[b] = total_ref[b] - jnp.where(there, all_ref[at, m : m + 1], 0.0)
    hidden = act_ref.shape[0]
    out_sum = jnp.zeros((hidden, lanes), jnp.float32)
    bias_sum = jnp.zeros((hidden, lanes), jnp.float32)
    grad = jnp.zeros((hidden, f_ref.shape[1]), jnp.float32)
    group = 4
    for c in range(blocks // group):
        highs = []
        lows = []
        for k in range(c * group, (c + 1) * group):
            act = act_ref[:, k * lanes : (k + 1) * lanes]
            node = total_ref[k] * scale
            weighted = act * node
            pre = node - weighted * act
            out_sum = out_sum + weighted
            bias_sum = bias_sum + pre
            high = pre.astype(jnp.bfloat16)
            highs.append(high)
            lows.append((pre - high.astype(jnp.float32)).astype(jnp.bfloat16))
        f = f_ref[c * group * lanes : (c + 1) * group * lanes]
        grad = grad + lax.dot_general(
            jnp.concatenate(highs, axis=1), f, NN, preferred_element_type=jnp.float32
        )
        grad = grad + lax.dot_general(
            jnp.concatenate(lows, axis=1), f, NN, preferred_element_type=jnp.float32
        )
    v = v_ref[...]
    parts = hidden // lanes
    for j in range(parts):
        span = slice(j * lanes, (j + 1) * lanes)
        turned = grad[span].T * v[:, span]
        for i in range(f_ref.shape[1] // 8):
            at = (i * parts + j) * 8
            grad_ref[at : at + 8] = turned[i * 8 : (i + 1) * 8]
    ones = jnp.ones((8, lanes), jnp.float32)
    across = lambda x: lax.dot_general(
        ones, x, NT, precision=lax.Precision.HIGHEST, preferred_element_type=jnp.float32
    )[:1]
    bias = across(bias_sum) * v
    out = across(out_sum)
    at = hidden * f_ref.shape[1] // lanes
    for j in range(parts):
        span = slice(j * lanes, (j + 1) * lanes)
        grad_ref[at + j : at + j + 1] = bias[:, span]
        grad_ref[at + parts + j : at + parts + j + 1] = out[:, span]
    grad_ref[at + 2 * parts :] = jnp.zeros_like(grad_ref[at + 2 * parts :])


def local(
    features, w_input, b_input, w_output, terminal, start_counts, visit_counts, dest_nodes,
    tile_rows, tile_cols, send_blocks, tile_weight,
):
    f32, bf16 = jnp.float32, jnp.bfloat16
    nodes, feat = features.shape
    tiles, lanes, _ = tile_weight.shape
    blocks = nodes // lanes
    rows = terminal.shape[0]
    hidden = w_input.shape[1]
    reach = send_blocks.shape[0] // 2
    width = send_blocks.shape[1]
    slots = 2 * reach * width
    count = lax.axis_size("dom")
    assert reach == 4 and count % 8 == 0
    shape = lambda *s: jax.ShapeDtypeStruct(s, f32)
    row_v = w_output[None, :]

    plan = Plan(blocks, tiles, slots, rows)
    like = lambda x: jax.ShapeDtypeStruct(x.shape, x.dtype)
    field = shape(blocks, rows, lanes)
    padded = shape(blocks + 1, rows, lanes)
    halves = jax.ShapeDtypeStruct((blocks, 2 * rows, lanes), bf16)
    parcel = shape(reach, width * rows, lanes)
    small = shape(reach, 8, lanes)
    all_s = pltpu.VMEM((4 * reach, width * rows, lanes), f32)
    ext_s = pltpu.VMEM((slots, 2 * rows, lanes), bf16)
    sum_s = pltpu.VMEM((blocks + 1, rows, lanes), f32)
    flow_s = pltpu.VMEM((slots + 1, rows, lanes), f32)
    bind = lambda kernel, *lead: functools.partial(kernel, *lead, reach, width)
    flops = 2 * tiles * lanes * lanes * 2 * rows
    moved = tiles * lanes * lanes * 2
    send_t = send_blocks.T
    row_b = b_input[None, :]

    z0, split, odd, even = call(
        bind(first_kernel),
        (field, halves, parcel, parcel),
        [
            pltpu.SMEM(send_t.shape, jnp.int32),
            pltpu.VMEM(terminal.shape, f32),
            pltpu.SemaphoreType.DMA((4,)),
            pltpu.SemaphoreType.DMA,
        ],
        (),
        (),
        flops,
        moved,
        hbm=(send_t, terminal),
    )

    def load(arrived):
        return call(
            functools.partial(load_kernel, plan),
            (
                jax.ShapeDtypeStruct((plan.size,), jnp.int32),
                *map(like, (tile_weight, features, w_input, row_b, row_v)),
            ),
            [
                pltpu.SMEM(tile_rows.shape, jnp.int32),
                pltpu.SMEM(tile_cols.shape, jnp.int32),
                pltpu.SMEM(send_t.shape, jnp.int32),
                pltpu.SMEM(dest_nodes.shape, jnp.int32),
                pltpu.SemaphoreType.DMA((5,)),
                pltpu.SemaphoreType.DMA((4,)),
            ],
            (),
            (),
            flops,
            moved,
            hbm=(tile_rows, tile_cols, send_t, dest_nodes, tile_weight, features, w_input, row_b, row_v),
            smem_out=True,
            after=(arrived,),
        )

    far, (plans, weight, feature, w_in, b_in, v_out) = exchange(odd, even, load)

    def near(split, forward, *after):
        kernel = functools.partial(near_kernel, plan, forward)
        return call(kernel, padded, [], (plans,), (weight, split), flops, moved, after=after)

    act, growth = call(
        network_kernel,
        (shape(hidden, nodes), shape(blocks, 1, lanes)),
        [],
        (),
        (w_in, b_in, v_out, feature),
        2 * nodes * hidden * feat,
        nodes * hidden * 4,
    )

    def backup(part, got):
        return call(
            bind(backup_kernel, plan),
            (field, halves, parcel, parcel),
            [all_s, ext_s, sum_s],
            (plans,),
            (weight, part, growth, *got),
            flops,
            moved,
        )

    z1, split, odd, even = backup(near(split, True), far)
    got, part = exchange(odd, even, lambda arrived: near(split, True, arrived))
    z2, split2, odd, even = backup(part, got)
    got, part = exchange(odd, even, lambda arrived: near(split2, True, arrived))
    values, split3, odd, even = call(
        bind(turn_kernel, plan),
        (shape(rows, nodes), halves, parcel, parcel),
        [all_s, ext_s, sum_s, flow_s],
        (plans,),
        (weight, part, growth, *got, start_counts),
        2 * flops,
        moved,
    )
    got, part = exchange(odd, even, lambda arrived: near(split3, False, arrived))
    u1, split4, odd, even = call(
        bind(spread_kernel, plan, count),
        (field, halves, parcel, parcel),
        [all_s, flow_s],
        (plans,),
        (weight, growth, part, *got),
        flops,
        moved,
    )
    got, part = exchange(odd, even, lambda arrived: near(split4, False, arrived))
    u2, split5, odd, even = call(
        bind(last_kernel, plan, count),
        (field, halves, small, small),
        [all_s, flow_s, all_s],
        (plans,),
        (weight, growth, part, *got, *far),
        flops,
        moved,
    )
    got, node = exchange(
        odd,
        even,
        lambda arrived: call(
            functools.partial(node_kernel, plan),
            shape(blocks, 1, lanes),
            [sum_s],
            (plans,),
            (weight, split5, z0, z1, z2, u1, u2, visit_counts),
            flops,
            moved,
            after=(arrived,),
        ),
    )
    every = ("dest", "dom")
    members = count * lax.axis_size("dest")
    used = hidden * feat // lanes + 2 * hidden // lanes
    share = -(-used // members)
    scale = 1.0 / math.sqrt(nodes * count * rows * lax.axis_size("dest"))
    packed = call(
        functools.partial(gradient_kernel, plan, count, reach, width, scale),
        shape(share * members, lanes),
        [pltpu.VMEM((blocks, 1, lanes), f32), pltpu.VMEM((4 * reach, 8, lanes), f32)],
        (plans,),
        (v_out, feature, act, node, *got),
        4 * nodes * hidden * feat,
        nodes * hidden * 4,
    )
    packed = packed.reshape(members, 1, share * lanes)
    mine = lax.all_to_all(packed, every, 0, 0, tiled=True).sum(axis=0, keepdims=True)
    spread = jnp.broadcast_to(mine, packed.shape)
    summed = lax.all_to_all(spread, every, 0, 0, tiled=True).reshape(share * members, lanes)
    side = summed[hidden * feat // lanes : used].reshape(2, hidden)
    grad = summed[: hidden * feat // lanes].reshape(feat // 8, hidden // lanes, 8, lanes)
    return values, grad.transpose(0, 2, 1, 3).reshape(feat, hidden), side[0], side[1]


def solution(mesh):
    in_specs = (
        P("dom", None),
        P(),
        P(),
        P(),
        P("dest", "dom"),
        P("dest", "dom"),
        P("dest", "dom"),
        P("dest"),
        P("dom"),
        P("dom"),
        P("dom", None),
        P("dom", None, None),
    )
    out_specs = (P("dest", "dom"), P(), P(), P())
    return jax.shard_map(local, mesh=mesh, in_specs=in_specs, out_specs=out_specs, check_vma=False)
```

```python
import functools
import math

import jax
import jax.numpy as jnp
from jax import lax
from jax.experimental import pallas as pl
from jax.experimental.pallas import tpu as pltpu
from jax.sharding import PartitionSpec as P

STEPS = 3
GOAL_GAIN = 32.0
VMEM_GRANT = 20 << 20

HOLD = lambda x: pltpu.with_memory_space_constraint(x, pltpu.HBM)
NT = (((1,), (1,)), ((), ()))
NN = (((1,), (0,)), ((), ()))


def offset_of(o, reach):
    return o - reach if o < reach else o - reach + 1


def present(me, count, shift):
    there = me + shift
    return jnp.logical_and(there >= 0, there < count)


def place(me, shift):
    origin = me - shift
    k = jnp.bitwise_xor(origin, me) & 3
    odd = (me >> 2) & 1
    apart = (origin >> 2) - (me >> 2)
    here = 2 * (k - 1) + (1 if shift > 0 else 0)
    below = jnp.where(odd == 1, 6, 10) + k
    above = jnp.where(odd == 1, 10, 6) + k
    return jnp.where(apart == 0, here, jnp.where(apart < 0, below, above))


PLACES = 14


def exchange(pairs, ends, work):
    me = lax.axis_index("dom")
    devices = range(lax.axis_size("dom"))
    group_even = (me // 4) % 2 == 0

    def partner(i):
        j = (i // 4 + (1 if (i // 4) % 2 == 1 else -1)) * 4 + i % 4
        return j if j in devices else i ^ 1

    flip = lambda x, bits: lax.ppermute(x, "dom", [(i, i ^ bits) for i in devices])
    near = [flip(pairs[k - 1], k) for k in (1, 2, 3)]
    near, done = lax.optimization_barrier((near, work()))
    up = jnp.stack([ends[1], *(x[1] for x in near)])
    down = jnp.stack([ends[0], *(x[0] for x in near)])
    first = flip(jnp.where(group_even, up, down), 4)
    second = lax.ppermute(
        jnp.where(group_even, down, up), "dom", [(i, partner(i)) for i in devices]
    )
    return (*near, first, second), done


def call(kernel, out_shape, scratch, smem, vmem, flops, moved, hbm=(), smem_out=False, after=()):
    space = lambda kind: pl.BlockSpec(memory_space=kind)
    out_specs = jax.tree.map(lambda _: space(pltpu.VMEM), out_shape)
    if smem_out:
        out_specs = (space(pltpu.SMEM), *out_specs[1:])
    if after:
        inner, lead, span = kernel, len(hbm) + len(smem) + len(vmem), len(after)
        kernel = lambda *refs: inner(*refs[:lead], *refs[lead + span :])
    hbm = [HOLD(x) for x in hbm]
    return pl.pallas_call(
        kernel,
        out_shape=out_shape,
        in_specs=[space(pltpu.HBM)] * len(hbm)
        + [space(pltpu.SMEM)] * len(smem)
        + [space(pltpu.VMEM)] * len(vmem)
        + [space(pl.ANY)] * len(after),
        out_specs=out_specs,
        scratch_shapes=scratch,
        compiler_params=pltpu.CompilerParams(vmem_limit_bytes=VMEM_GRANT),
        cost_estimate=pl.CostEstimate(flops=flops, bytes_accessed=moved, transcendentals=0),
    )(*hbm, *smem, *vmem, *after)


def store_split(ref, k, x):
    rows = x.shape[0]
    high = x.astype(jnp.bfloat16)
    low = (x - high.astype(jnp.float32)).astype(jnp.bfloat16)
    ref[k, :rows] = high
    ref[k, rows:] = low


def product(lhs, rhs, dims):
    both = lax.dot_general(lhs, rhs, dims, preferred_element_type=jnp.float32)
    rows = both.shape[0] // 2
    return both[:rows] + both[rows:]


def offsets(reach):
    return [offset_of(o, reach) for o in range(2 * reach)]


def send_items(pairs, ends_ref, reach, sign, item):
    core = lax.axis_index("dom") & 1
    for o, f in enumerate(offsets(reach)):
        shift = sign * f
        side = 1 if shift > 0 else 0
        if abs(shift) == reach:
            item(o, ends_ref, (side,))
        elif shift % 2 == 0:
            item(o, pairs, (1, side))
        else:
            first = shift in (-3, 1)
            item(o, pairs, (2 * core if first else 2 - 2 * core, side))


def send_slots(width, source):
    def item(o, ref, at):
        for m in range(width):
            piece = source(o, m)
            rows = piece.shape[0]
            ref[(*at, slice(m * rows, (m + 1) * rows))] = piece

    return item


def collect(all_ref, parts):
    at = 0
    for part in parts:
        for k in range(part.shape[0]):
            all_ref[at] = part[k]
            at += 1


class Plan:
    def __init__(self, blocks, tiles, slots, rows):
        at = 0
        for name, size in (
            ("far_t", slots), ("far_r", slots), ("far_c", slots),
            ("near_t", tiles - blocks), ("near_r", tiles - blocks), ("near_c", tiles - blocks),
            ("send", slots), ("dest", rows), ("near", 1), ("far", 1),
        ):
            setattr(self, name, at)
            at += size
        self.size = at
        self.blocks, self.slots, self.extra = blocks, slots, tiles - blocks


def load_kernel(
    plan, rows_hbm, cols_hbm, send_hbm, dest_hbm, tile_hbm, f_hbm, w_hbm, b_hbm, v_hbm,
    plan_ref, tile_ref, f_ref, w_ref, b_ref, v_ref, rows_ref, cols_ref, send_ref, dest_ref, sem, small,
):
    smalls = [
        pltpu.make_async_copy(src, dst, small.at[k])
        for k, (src, dst) in enumerate(
            ((rows_hbm, rows_ref), (cols_hbm, cols_ref), (send_hbm, send_ref), (dest_hbm, dest_ref))
        )
    ]
    larges = [
        pltpu.make_async_copy(src, dst, sem.at[k])
        for k, (src, dst) in enumerate(
            ((f_hbm, f_ref), (w_hbm, w_ref), (b_hbm, b_ref), (v_hbm, v_ref), (tile_hbm, tile_ref))
        )
    ]
    for copy in smalls + larges:
        copy.start()
    for copy in smalls:
        copy.wait()
    for k in range(plan.size):
        plan_ref[k] = 0
    width = send_ref.shape[0]
    for k in range(plan.slots):
        plan_ref[plan.far_c + k] = plan.blocks
        plan_ref[plan.send + k] = send_ref[k % width, k // width]
    for k in range(dest_ref.shape[0]):
        plan_ref[plan.dest + k] = dest_ref[k]

    def sort_tile(k, counts):
        near, far = counts
        t = plan.blocks + k
        r, c = rows_ref[t], cols_ref[t]
        apart = c >= plan.blocks
        at = jnp.where(apart, plan.far_t + far, plan.near_t + near)
        step = jnp.where(apart, plan.slots, plan.extra)
        plan_ref[at] = t
        plan_ref[at + step] = r
        plan_ref[at + 2 * step] = c
        one = apart.astype(jnp.int32)
        return near + 1 - one, far + one

    near, far = lax.fori_loop(0, plan.extra, sort_tile, (jnp.int32(0), jnp.int32(0)))
    plan_ref[plan.near] = near
    plan_ref[plan.far] = far
    for copy in larges:
        copy.wait()


def network_kernel(w_ref, b_ref, v_ref, f_ref, act_ref, growth_ref):
    lanes = growth_ref.shape[2]
    hidden = act_ref.shape[0]
    group = 2
    w = w_ref[...].T
    b = jnp.broadcast_to(b_ref[...], (lanes, hidden)).T
    v = jnp.broadcast_to(v_ref[...], (lanes, hidden)).T
    for c in range(growth_ref.shape[0] // group):
        f = f_ref[c * group * lanes : (c + 1) * group * lanes]
        pre = lax.dot_general(w, f, NT, preferred_element_type=jnp.float32)
        for k in range(group):
            at = c * group + k
            act = jnp.tanh(pre[:, k * lanes : (k + 1) * lanes] + b)
            act_ref[:, at * lanes : (at + 1) * lanes] = act
            growth_ref[at] = jnp.exp(jnp.sum(act * v, axis=0, keepdims=True))


def first_kernel(
    reach, width, send_hbm, term_hbm, z_ref, split_ref, pairs_ref, ends_ref, send_ref, term_ref, sem, small
):
    blocks, _, lanes = z_ref.shape
    parts = sem.shape[0]
    span = blocks // parts
    asked = pltpu.make_async_copy(send_hbm, send_ref, small)
    cut = lambda ref, i: ref.at[:, i * span * lanes : (i + 1) * span * lanes]
    copies = [
        pltpu.make_async_copy(cut(term_hbm, i), cut(term_ref, i), sem.at[i]) for i in range(parts)
    ]
    asked.start()
    for copy in copies:
        copy.start()
    for i, copy in enumerate(copies):
        copy.wait()
        for k in range(i * span, (i + 1) * span):
            z = jnp.exp(term_ref[:, k * lanes : (k + 1) * lanes])
            z_ref[k] = z
            store_split(split_ref, k, z)
    asked.wait()
    send_items(
        pairs_ref, ends_ref, reach, 1, send_slots(width, lambda o, m: z_ref[send_ref[m, o]])
    )


def near_products(plan, plan_ref, w_ref, split_ref, sum_ref, forward):
    dims = NT if forward else NN
    for k in range(plan.blocks):
        sum_ref[k] = product(split_ref[k], w_ref[k], dims)
    count = plan_ref[plan.near]
    for k in range(plan.extra):
        r, c = plan_ref[plan.near_r + k], plan_ref[plan.near_c + k]
        source, into = (c, r) if forward else (r, c)
        into = jnp.where(k < count, into, plan.blocks)
        sum_ref[into] = sum_ref[into] + product(
            split_ref[source], w_ref[plan_ref[plan.near_t + k]], dims
        )


def near_kernel(plan, forward, plan_ref, w_ref, split_ref, sum_ref):
    near_products(plan, plan_ref, w_ref, split_ref, sum_ref, forward)


def backed_up(
    plan, reach, width, plan_ref, w_ref, part_ref, parts, all_ref, ext_ref, sum_ref
):
    rows = part_ref.shape[1]
    me = lax.axis_index("dom")
    collect(all_ref, parts)
    for o, f in enumerate(offsets(reach)):
        at = place(me, f)
        for m in range(width):
            store_split(ext_ref, o * width + m, all_ref[at, m * rows : (m + 1) * rows])
    for k in range(plan.blocks):
        sum_ref[k] = part_ref[k]
    count = plan_ref[plan.far]
    for k in range(plan.slots):
        slot = plan_ref[plan.far_c + k] - plan.blocks
        into = jnp.where(k < count, plan_ref[plan.far_r + k], plan.blocks)
        sum_ref[into] = sum_ref[into] + product(
            ext_ref[slot], w_ref[plan_ref[plan.far_t + k]], NT
        )


def goal_of(plan, plan_ref, rows, lanes):
    row = lax.broadcasted_iota(jnp.int32, (rows, lanes), 0)
    dest = jnp.zeros((rows, lanes), jnp.int32)
    for d in range(rows):
        dest = jnp.where(row == d, plan_ref[plan.dest + d], dest)
    return dest


def with_goal(k, blocks, growth_ref, sum_ref, dest, me):
    _, rows, lanes = sum_ref.shape
    node = (me * blocks + k) * lanes + lax.broadcasted_iota(jnp.int32, (rows, lanes), 1)
    return growth_ref[k] * sum_ref[k] + jnp.where(node == dest, GOAL_GAIN, 0.0)


def backup_kernel(
    plan, reach, width, plan_ref, w_ref, part_ref, growth_ref,
    got1, got2, got3, got4, got5,
    z_ref, next_ref, pairs_ref, ends_ref, all_ref, ext_ref, sum_ref,
):
    blocks, rows, lanes = z_ref.shape
    me = lax.axis_index("dom")
    backed_up(
        plan, reach, width, plan_ref, w_ref, part_ref,
        (got1, got2, got3, got4, got5), all_ref, ext_ref, sum_ref,
    )
    dest = goal_of(plan, plan_ref, rows, lanes)
    for k in range(blocks):
        z = with_goal(k, blocks, growth_ref, sum_ref, dest, me)
        z_ref[k] = z
        store_split(next_ref, k, z)
    send_items(
        pairs_ref, ends_ref, reach, 1,
        send_slots(width, lambda o, m: z_ref[plan_ref[plan.send + o * width + m]]),
    )


def far_flows(plan, plan_ref, w_ref, split_ref, flow_ref):
    for k in range(plan.slots + 1):
        flow_ref[k] = jnp.zeros(flow_ref.shape[1:], jnp.float32)
    count = plan_ref[plan.far]
    for k in range(plan.slots):
        slot = plan_ref[plan.far_c + k] - plan.blocks
        into = jnp.where(k < count, slot, plan.slots)
        flow_ref[into] = flow_ref[into] + product(
            split_ref[plan_ref[plan.far_r + k]], w_ref[plan_ref[plan.far_t + k]], NN
        )


def turn_kernel(
    plan, reach, width, plan_ref, w_ref, part_ref, growth_ref,
    got1, got2, got3, got4, got5, start_ref,
    z_ref, next_ref, pairs_ref, ends_ref, all_ref, ext_ref, sum_ref, flow_ref,
):
    blocks = plan.blocks
    _, rows, lanes = part_ref.shape
    me = lax.axis_index("dom")
    backed_up(
        plan, reach, width, plan_ref, w_ref, part_ref,
        (got1, got2, got3, got4, got5), all_ref, ext_ref, sum_ref,
    )
    dest = goal_of(plan, plan_ref, rows, lanes)
    for k in range(blocks):
        z = with_goal(k, blocks, growth_ref, sum_ref, dest, me)
        span = slice(k * lanes, (k + 1) * lanes)
        z_ref[k] = z
        store_split(next_ref, k, growth_ref[k] * start_ref[:, span].astype(jnp.float32) / z)
    far_flows(plan, plan_ref, w_ref, next_ref, flow_ref)
    send_items(
        pairs_ref, ends_ref, reach, -1, send_slots(width, lambda o, m: flow_ref[o * width + m])
    )


def flows(
    plan, count, reach, width, plan_ref, w_ref, growth_ref, sum_ref, parts,
    u_ref, next_ref, all_ref, flow_ref,
):
    blocks, rows, _ = u_ref.shape
    me = lax.axis_index("dom")
    for k in range(blocks):
        u_ref[k] = sum_ref[k]
    collect(all_ref, parts)
    for o, f in enumerate(offsets(reach)):
        there = present(me, count, f)
        at = place(me, -f)
        for m in range(width):
            b = plan_ref[plan.send + o * width + m]
            piece = all_ref[at, m * rows : (m + 1) * rows]
            u_ref[b] = u_ref[b] + jnp.where(there, piece, 0.0)
    for k in range(blocks):
        store_split(next_ref, k, growth_ref[k] * u_ref[k])
    far_flows(plan, plan_ref, w_ref, next_ref, flow_ref)


def spread_kernel(
    plan, count, reach, width, plan_ref, w_ref, growth_ref, sum_ref,
    got1, got2, got3, got4, got5,
    u_ref, next_ref, pairs_ref, ends_ref, all_ref, flow_ref,
):
    flows(
        plan, count, reach, width, plan_ref, w_ref, growth_ref, sum_ref,
        (got1, got2, got3, got4, got5), u_ref, next_ref, all_ref, flow_ref,
    )
    send_items(
        pairs_ref, ends_ref, reach, -1, send_slots(width, lambda o, m: flow_ref[o * width + m])
    )


def last_kernel(
    plan, count, reach, width, plan_ref, w_ref, growth_ref, sum_ref,
    got1, got2, got3, got4, got5, z1_got, z2_got, z3_got, z4_got, z5_got,
    u_ref, next_ref, pairs_ref, ends_ref, all_ref, flow_ref, far_ref,
):
    rows = u_ref.shape[1]
    me = lax.axis_index("dom")
    flows(
        plan, count, reach, width, plan_ref, w_ref, growth_ref, sum_ref,
        (got1, got2, got3, got4, got5), u_ref, next_ref, all_ref, flow_ref,
    )
    collect(far_ref, (z1_got, z2_got, z3_got, z4_got, z5_got))
    row = lax.broadcasted_iota(jnp.int32, ends_ref.shape[1:], 0)

    def item(o, ref, where):
        at = place(me, offset_of(o, reach))
        sums = jnp.zeros(ends_ref.shape[1:], jnp.float32)
        for m in range(width):
            lost = far_ref[at, m * rows : (m + 1) * rows] * flow_ref[o * width + m]
            sums = jnp.where(row == m, jnp.sum(lost, axis=0, keepdims=True), sums)
        ref[where] = sums

    send_items(pairs_ref, ends_ref, reach, -1, item)


def node_kernel(
    plan, plan_ref, w_ref, split_ref, z0_ref, z1_ref, z2_ref, u1_ref, u2_ref, visit_ref,
    node_ref, sum_ref,
):
    blocks, _, lanes = z0_ref.shape
    near_products(plan, plan_ref, w_ref, split_ref, sum_ref, False)
    for k in range(blocks):
        left = (
            visit_ref[:, k * lanes : (k + 1) * lanes].astype(jnp.float32)
            - z2_ref[k] * u1_ref[k]
            - z1_ref[k] * u2_ref[k]
            - z0_ref[k] * sum_ref[k]
        )
        node_ref[k] = jnp.sum(left, axis=0, keepdims=True)


def gradient_kernel(
    plan, count, reach, width, scale, plan_ref, v_ref, f_ref, act_ref, node_ref,
    got1, got2, got3, got4, got5, packed_ref, total_ref, all_ref,
):
    blocks, _, lanes = node_ref.shape
    me = lax.axis_index("dom")
    collect(all_ref, (got1, got2, got3, got4, got5))
    for k in range(blocks):
        total_ref[k] = node_ref[k]
    for o, f in enumerate(offsets(reach)):
        there = present(me, count, f)
        at = place(me, -f)
        for m in range(width):
            b = plan_ref[plan.send + o * width + m]
            total_ref[b] = total_ref[b] - jnp.where(there, all_ref[at, m : m + 1], 0.0)
    hidden = act_ref.shape[0]
    out_sum = jnp.zeros((hidden, lanes), jnp.float32)
    bias_sum = jnp.zeros((hidden, lanes), jnp.float32)
    grad = jnp.zeros((hidden, f_ref.shape[1]), jnp.float32)
    group = 4
    for c in range(blocks // group):
        highs = []
        lows = []
        for k in range(c * group, (c + 1) * group):
            act = act_ref[:, k * lanes : (k + 1) * lanes]
            node = total_ref[k] * scale
            weighted = act * node
            pre = node - weighted * act
            out_sum = out_sum + weighted
            bias_sum = bias_sum + pre
            high = pre.astype(jnp.bfloat16)
            highs.append(high)
            lows.append((pre - high.astype(jnp.float32)).astype(jnp.bfloat16))
        f = f_ref[c * group * lanes : (c + 1) * group * lanes]
        grad = grad + lax.dot_general(
            jnp.concatenate(highs, axis=1), f, NN, preferred_element_type=jnp.float32
        )
        grad = grad + lax.dot_general(
            jnp.concatenate(lows, axis=1), f, NN, preferred_element_type=jnp.float32
        )
    v = v_ref[...]
    core = me & 1
    half = packed_ref.shape[1]
    parts = hidden // lanes
    tall = hidden * f_ref.shape[1] // lanes

    def put(at, rows):
        packed_ref[jnp.bitwise_xor(core, at // half), at % half : at % half + rows.shape[0]] = rows

    for j in range(parts):
        span = slice(j * lanes, (j + 1) * lanes)
        turned = grad[span].T * v[:, span]
        for i in range(f_ref.shape[1] // 8):
            put((i * parts + j) * 8, turned[i * 8 : (i + 1) * 8])
    ones = jnp.ones((8, lanes), jnp.float32)
    across = lambda x: lax.dot_general(
        ones, x, NT, precision=lax.Precision.HIGHEST, preferred_element_type=jnp.float32
    )[:1]
    bias, out = across(bias_sum) * v, across(out_sum)
    cut = lambda x: [x[:, j * lanes : (j + 1) * lanes] for j in range(parts)]
    put(tall, jnp.concatenate(cut(bias) + cut(out), axis=0))
    for at in range(tall + 2 * parts, 2 * half, 8):
        put(at, jnp.zeros((8, lanes), jnp.float32))


def finish_kernel(mine_ref, other_ref, grad_hbm, bias_hbm, out_hbm, both_ref, bias_ref, out_ref, sem):
    half = mine_ref.shape[0]
    tall, parts = grad_hbm.shape[0], bias_hbm.shape[0]
    core = lax.axis_index("dom") & 1
    both_ref[core] = mine_ref[...]
    both_ref[1 - core] = other_ref[...]
    which, at = tall // half, tall % half
    bias_ref[...] = both_ref[which, at : at + parts]
    out_ref[...] = both_ref[which, at + parts : at + 2 * parts]
    pieces = [(bias_ref, bias_hbm), (out_ref, out_hbm)]
    for h in range(2):
        start, stop = h * half, min((h + 1) * half, tall)
        if start < stop:
            pieces.append((both_ref.at[h, : stop - start], grad_hbm.at[start:stop]))
    copies = [pltpu.make_async_copy(src, dst, sem.at[k]) for k, (src, dst) in enumerate(pieces)]
    for copy in copies:
        copy.start()
    for copy in copies:
        copy.wait()


def values_kernel(z_ref, values_ref):
    blocks, _, lanes = z_ref.shape
    for k in range(blocks):
        values_ref[:, k * lanes : (k + 1) * lanes] = jnp.log(z_ref[k])


def local(
    features, w_input, b_input, w_output, terminal, start_counts, visit_counts, dest_nodes,
    tile_rows, tile_cols, send_blocks, tile_weight,
):
    f32, bf16 = jnp.float32, jnp.bfloat16
    nodes, feat = features.shape
    tiles, lanes, _ = tile_weight.shape
    blocks = nodes // lanes
    rows = terminal.shape[0]
    hidden = w_input.shape[1]
    reach = send_blocks.shape[0] // 2
    width = send_blocks.shape[1]
    slots = 2 * reach * width
    count = lax.axis_size("dom")
    assert reach == 4 and count % 8 == 0
    shape = lambda *s: jax.ShapeDtypeStruct(s, f32)
    row_v = w_output[None, :]

    plan = Plan(blocks, tiles, slots, rows)
    like = lambda x: jax.ShapeDtypeStruct(x.shape, x.dtype)
    field = shape(blocks, rows, lanes)
    padded = shape(blocks + 1, rows, lanes)
    halves = jax.ShapeDtypeStruct((blocks, 2 * rows, lanes), bf16)
    parcels = (shape(3, 2, width * rows, lanes), shape(2, width * rows, lanes))
    smalls = (shape(3, 2, 8, lanes), shape(2, 8, lanes))
    all_s = pltpu.VMEM((PLACES, width * rows, lanes), f32)
    ext_s = pltpu.VMEM((slots, 2 * rows, lanes), bf16)
    sum_s = pltpu.VMEM((blocks + 1, rows, lanes), f32)
    flow_s = pltpu.VMEM((slots + 1, rows, lanes), f32)
    bind = lambda kernel, *lead: functools.partial(kernel, *lead, reach, width)
    flops = 2 * tiles * lanes * lanes * 2 * rows
    moved = tiles * lanes * lanes * 2
    send_t = send_blocks.T
    row_b = b_input[None, :]

    z0, split, pairs, ends = call(
        bind(first_kernel),
        (field, halves, *parcels),
        [
            pltpu.SMEM(send_t.shape, jnp.int32),
            pltpu.VMEM(terminal.shape, f32),
            pltpu.SemaphoreType.DMA((4,)),
            pltpu.SemaphoreType.DMA,
        ],
        (),
        (),
        flops,
        moved,
        hbm=(send_t, terminal),
    )

    def load():
        return call(
            functools.partial(load_kernel, plan),
            (
                jax.ShapeDtypeStruct((plan.size,), jnp.int32),
                *map(like, (tile_weight, features, w_input, row_b, row_v)),
            ),
            [
                pltpu.SMEM(tile_rows.shape, jnp.int32),
                pltpu.SMEM(tile_cols.shape, jnp.int32),
                pltpu.SMEM(send_t.shape, jnp.int32),
                pltpu.SMEM(dest_nodes.shape, jnp.int32),
                pltpu.SemaphoreType.DMA((5,)),
                pltpu.SemaphoreType.DMA((4,)),
            ],
            (),
            (),
            flops,
            moved,
            hbm=(tile_rows, tile_cols, send_t, dest_nodes, tile_weight, features, w_input, row_b, row_v),
            smem_out=True,
            after=(ends,),
        )

    far, (plans, weight, feature, w_in, b_in, v_out) = exchange(pairs, ends, load)

    def near(split, forward):
        kernel = functools.partial(near_kernel, plan, forward)
        return call(kernel, padded, [], (plans,), (weight, split), flops, moved)

    act, growth = call(
        network_kernel,
        (shape(hidden, nodes), shape(blocks, 1, lanes)),
        [],
        (),
        (w_in, b_in, v_out, feature),
        2 * nodes * hidden * feat,
        nodes * hidden * 4,
    )

    def backup(part, got):
        return call(
            bind(backup_kernel, plan),
            (field, halves, *parcels),
            [all_s, ext_s, sum_s],
            (plans,),
            (weight, part, growth, *got),
            flops,
            moved,
        )

    z1, split, pairs, ends = backup(near(split, True), far)
    got, part = exchange(pairs, ends, lambda: near(split, True))
    z2, split2, pairs, ends = backup(part, got)
    got, part = exchange(pairs, ends, lambda: near(split2, True))
    z3, split3, pairs, ends = call(
        bind(turn_kernel, plan),
        (field, halves, *parcels),
        [all_s, ext_s, sum_s, flow_s],
        (plans,),
        (weight, part, growth, *got, start_counts),
        2 * flops,
        moved,
    )
    values = call(values_kernel, shape(rows, nodes), [], (), (z3,), flops // 8, nodes * rows * 8)
    got, part = exchange(pairs, ends, lambda: near(split3, False))
    u1, split4, pairs, ends = call(
        bind(spread_kernel, plan, count),
        (field, halves, *parcels),
        [all_s, flow_s],
        (plans,),
        (weight, growth, part, *got),
        flops,
        moved,
    )
    got, part = exchange(pairs, ends, lambda: near(split4, False))
    u2, split5, pairs, ends = call(
        bind(last_kernel, plan, count),
        (field, halves, *smalls),
        [all_s, flow_s, all_s],
        (plans,),
        (weight, growth, part, *got, *far),
        flops,
        moved,
    )
    got, node = exchange(
        pairs,
        ends,
        lambda: call(
            functools.partial(node_kernel, plan),
            shape(blocks, 1, lanes),
            [sum_s],
            (plans,),
            (weight, split5, z0, z1, z2, u1, u2, visit_counts),
            flops,
            moved,
        ),
    )
    every = ("dest", "dom")
    members = count * lax.axis_size("dest")
    tall = hidden * feat // lanes
    share = -(-(tall + 2 * hidden // lanes) // members)
    half = share * members // 2
    scale = 1.0 / math.sqrt(nodes * count * rows * lax.axis_size("dest"))
    packed = call(
        functools.partial(gradient_kernel, plan, count, reach, width, scale),
        shape(2, half, lanes),
        [
            pltpu.VMEM((blocks, 1, lanes), f32),
            pltpu.VMEM((PLACES, 8, lanes), f32),
        ],
        (plans,),
        (v_out, feature, act, node, *got),
        4 * nodes * hidden * feat,
        nodes * hidden * 4,
    )
    twins = [(i, i ^ 1) for i in range(count)]
    mine = packed[0] + lax.ppermute(packed[1], "dom", twins)
    same_core = [[i for i in range(members) if i % 2 == core] for core in range(2)]
    swap = lambda x: lax.all_to_all(x, every, 0, 0, tiled=True, axis_index_groups=same_core)
    mine = mine.reshape(members // 2, 1, share * lanes)
    mine = jnp.broadcast_to(swap(mine).sum(axis=0, keepdims=True), mine.shape)
    mine = swap(mine).reshape(half, lanes)
    other = lax.ppermute(mine, "dom", twins)
    in_hbm = pl.BlockSpec(memory_space=pltpu.HBM)
    in_vmem = pl.BlockSpec(memory_space=pltpu.VMEM)
    parts = hidden // lanes
    grad, bias, out = pl.pallas_call(
        finish_kernel,
        out_shape=(shape(tall, lanes), shape(parts, lanes), shape(parts, lanes)),
        in_specs=[in_vmem] * 2,
        out_specs=[in_hbm] * 3,
        scratch_shapes=[
            pltpu.VMEM((2, half, lanes), f32),
            pltpu.VMEM((parts, lanes), f32),
            pltpu.VMEM((parts, lanes), f32),
            pltpu.SemaphoreType.DMA((4,)),
        ],
        compiler_params=pltpu.CompilerParams(vmem_limit_bytes=VMEM_GRANT),
    )(mine, other)
    grad = grad.reshape(feat // 8, parts, 8, lanes).transpose(0, 2, 1, 3).reshape(feat, hidden)
    return values, grad, bias.reshape(-1), out.reshape(-1)


def solution(mesh):
    in_specs = (
        P("dom", None),
        P(),
        P(),
        P(),
        P("dest", "dom"),
        P("dest", "dom"),
        P("dest", "dom"),
        P("dest"),
        P("dom"),
        P("dom"),
        P("dom", None),
        P("dom", None, None),
    )
    out_specs = (P("dest", "dom"), P(), P(), P())
    return jax.shard_map(local, mesh=mesh, in_specs=in_specs, out_specs=out_specs, check_vma=False)
```

```python
import functools
import math

import jax
import jax.numpy as jnp
from jax import lax
from jax.experimental import pallas as pl
from jax.experimental.pallas import tpu as pltpu
from jax.sharding import PartitionSpec as P

STEPS = 3
GOAL_GAIN = 32.0
VMEM_GRANT = 20 << 20

HOLD = lambda x: pltpu.with_memory_space_constraint(x, pltpu.HBM)
NT = (((1,), (1,)), ((), ()))
NN = (((1,), (0,)), ((), ()))


def offset_of(o, reach):
    return o - reach if o < reach else o - reach + 1


def present(me, count, shift):
    there = me + shift
    return jnp.logical_and(there >= 0, there < count)


def place(me, shift):
    origin = me - shift
    k = jnp.bitwise_xor(origin, me) & 3
    odd = (me >> 2) & 1
    apart = (origin >> 2) - (me >> 2)
    here = 2 * (k - 1) + (1 if shift > 0 else 0)
    below = jnp.where(odd == 1, 6, 10) + k
    above = jnp.where(odd == 1, 10, 6) + k
    return jnp.where(apart == 0, here, jnp.where(apart < 0, below, above))


PLACES = 14


def exchange(pairs, ends, work):
    me = lax.axis_index("dom")
    devices = range(lax.axis_size("dom"))
    group_even = (me // 4) % 2 == 0

    def partner(i):
        j = (i // 4 + (1 if (i // 4) % 2 == 1 else -1)) * 4 + i % 4
        return j if j in devices else i ^ 1

    flip = lambda x, bits: lax.ppermute(x, "dom", [(i, i ^ bits) for i in devices])
    near = [flip(pairs[k - 1], k) for k in (1, 2, 3)]
    near, done = lax.optimization_barrier((near, work()))
    up = jnp.stack([ends[1], *(x[1] for x in near)])
    down = jnp.stack([ends[0], *(x[0] for x in near)])
    first = flip(jnp.where(group_even, up, down), 4)
    second = lax.ppermute(
        jnp.where(group_even, down, up), "dom", [(i, partner(i)) for i in devices]
    )
    return (*near, first, second), done


class Column:
    def __init__(self, ref):
        self.ref = ref

    def __getitem__(self, k):
        return self.ref[k, 0]


def call(kernel, out_shape, scratch, plans, vmem, flops, moved, hbm=(), after=()):
    space = lambda kind: pl.BlockSpec(memory_space=kind)
    out_specs = jax.tree.map(lambda _: space(pltpu.VMEM), out_shape)
    inner, at, lead = kernel, len(hbm), len(hbm) + len(plans)
    stop, span = lead + len(vmem), len(after)

    def kernel(*refs):
        columns = [Column(ref) for ref in refs[at:lead]]
        inner(*refs[:at], *columns, *refs[lead:stop], *refs[stop + span :])

    hbm = [HOLD(x) for x in hbm]
    return pl.pallas_call(
        kernel,
        out_shape=out_shape,
        in_specs=[space(pltpu.HBM)] * len(hbm)
        + [space(pltpu.VMEM)] * (len(plans) + len(vmem))
        + [space(pl.ANY)] * len(after),
        out_specs=out_specs,
        scratch_shapes=scratch,
        compiler_params=pltpu.CompilerParams(vmem_limit_bytes=VMEM_GRANT),
        cost_estimate=pl.CostEstimate(flops=flops, bytes_accessed=moved, transcendentals=0),
    )(*hbm, *plans, *vmem, *after)


def store_split(ref, k, x):
    rows = x.shape[0]
    high = x.astype(jnp.bfloat16)
    low = (x - high.astype(jnp.float32)).astype(jnp.bfloat16)
    ref[k, :rows] = high
    ref[k, rows:] = low


def product(lhs, rhs, dims):
    both = lax.dot_general(lhs, rhs, dims, preferred_element_type=jnp.float32)
    rows = both.shape[0] // 2
    return both[:rows] + both[rows:]


def offsets(reach):
    return [offset_of(o, reach) for o in range(2 * reach)]


def send_items(pairs, ends_ref, reach, sign, item):
    core = lax.axis_index("dom") & 1
    for o, f in enumerate(offsets(reach)):
        shift = sign * f
        side = 1 if shift > 0 else 0
        if abs(shift) == reach:
            item(o, ends_ref, (side,))
        elif shift % 2 == 0:
            item(o, pairs, (1, side))
        else:
            first = shift in (-3, 1)
            item(o, pairs, (2 * core if first else 2 - 2 * core, side))


def send_slots(width, source):
    def item(o, ref, at):
        for m in range(width):
            piece = source(o, m)
            rows = piece.shape[0]
            ref[(*at, slice(m * rows, (m + 1) * rows))] = piece

    return item


def collect(all_ref, parts):
    at = 0
    for part in parts:
        for k in range(part.shape[0]):
            all_ref[at] = part[k]
            at += 1


class Plan:
    def __init__(self, blocks, tiles, slots, rows):
        at = 0
        for name, size in (
            ("far_t", slots), ("far_r", slots), ("far_c", slots),
            ("near_t", tiles - blocks), ("near_r", tiles - blocks), ("near_c", tiles - blocks),
            ("send", slots), ("dest", rows), ("near", 1), ("far", 1),
        ):
            setattr(self, name, at)
            at += size
        self.size = at
        self.blocks, self.slots, self.extra = blocks, slots, tiles - blocks


def load_kernel(
    plan, rows_hbm, cols_hbm, send_hbm, dest_hbm, tile_hbm, f_hbm, w_hbm, b_hbm, v_hbm,
    table_ref, tile_ref, f_ref, w_ref, b_ref, v_ref,
    plan_ref, rows_ref, cols_ref, send_ref, dest_ref, sem, small,
):
    smalls = [
        pltpu.make_async_copy(src, dst, small.at[k])
        for k, (src, dst) in enumerate(
            ((rows_hbm, rows_ref), (cols_hbm, cols_ref), (send_hbm, send_ref), (dest_hbm, dest_ref))
        )
    ]
    larges = [
        pltpu.make_async_copy(src, dst, sem.at[k])
        for k, (src, dst) in enumerate(
            ((f_hbm, f_ref), (w_hbm, w_ref), (b_hbm, b_ref), (v_hbm, v_ref), (tile_hbm, tile_ref))
        )
    ]
    for copy in smalls + larges:
        copy.start()
    for copy in smalls:
        copy.wait()
    for k in range(plan.size):
        plan_ref[k] = 0
    width = send_ref.shape[0]
    for k in range(plan.slots):
        plan_ref[plan.far_c + k] = plan.blocks
        plan_ref[plan.send + k] = send_ref[k % width, k // width]
    for k in range(dest_ref.shape[0]):
        plan_ref[plan.dest + k] = dest_ref[k]

    def sort_tile(k, counts):
        near, far = counts
        t = plan.blocks + k
        r, c = rows_ref[t], cols_ref[t]
        apart = c >= plan.blocks
        at = jnp.where(apart, plan.far_t + far, plan.near_t + near)
        step = jnp.where(apart, plan.slots, plan.extra)
        plan_ref[at] = t
        plan_ref[at + step] = r
        plan_ref[at + 2 * step] = c
        one = apart.astype(jnp.int32)
        return near + 1 - one, far + one

    near, far = lax.fori_loop(0, plan.extra, sort_tile, (jnp.int32(0), jnp.int32(0)))
    plan_ref[plan.near] = near
    plan_ref[plan.far] = far
    for k in range(plan.size):
        table_ref[k : k + 1] = jnp.full((1, table_ref.shape[1]), plan_ref[k], jnp.int32)
    for copy in larges:
        copy.wait()


def network_kernel(w_ref, b_ref, v_ref, f_ref, act_ref, growth_ref):
    lanes = growth_ref.shape[2]
    hidden = act_ref.shape[0]
    group = 2
    w = w_ref[...].T
    b = jnp.broadcast_to(b_ref[...], (lanes, hidden)).T
    v = jnp.broadcast_to(v_ref[...], (lanes, hidden)).T
    for c in range(growth_ref.shape[0] // group):
        f = f_ref[c * group * lanes : (c + 1) * group * lanes]
        pre = lax.dot_general(w, f, NT, preferred_element_type=jnp.float32)
        for k in range(group):
            at = c * group + k
            act = jnp.tanh(pre[:, k * lanes : (k + 1) * lanes] + b)
            act_ref[:, at * lanes : (at + 1) * lanes] = act
            growth_ref[at] = jnp.exp(jnp.sum(act * v, axis=0, keepdims=True))


def first_kernel(
    reach, width, send_hbm, term_hbm, z_ref, split_ref, pairs_ref, ends_ref, send_ref, term_ref, sem, small
):
    blocks, _, lanes = z_ref.shape
    parts = sem.shape[0]
    span = blocks // parts
    asked = pltpu.make_async_copy(send_hbm, send_ref, small)
    cut = lambda ref, i: ref.at[:, i * span * lanes : (i + 1) * span * lanes]
    copies = [
        pltpu.make_async_copy(cut(term_hbm, i), cut(term_ref, i), sem.at[i]) for i in range(parts)
    ]
    asked.start()
    for copy in copies:
        copy.start()
    for i, copy in enumerate(copies):
        copy.wait()
        for k in range(i * span, (i + 1) * span):
            z = jnp.exp(term_ref[:, k * lanes : (k + 1) * lanes])
            z_ref[k] = z
            store_split(split_ref, k, z)
    asked.wait()
    send_items(
        pairs_ref, ends_ref, reach, 1, send_slots(width, lambda o, m: z_ref[send_ref[m, o]])
    )


def near_products(plan, plan_ref, w_ref, split_ref, sum_ref, forward):
    dims = NT if forward else NN
    for k in range(plan.blocks):
        sum_ref[k] = product(split_ref[k], w_ref[k], dims)
    count = plan_ref[plan.near]
    for k in range(plan.extra):
        r, c = plan_ref[plan.near_r + k], plan_ref[plan.near_c + k]
        source, into = (c, r) if forward else (r, c)
        into = jnp.where(k < count, into, plan.blocks)
        sum_ref[into] = sum_ref[into] + product(
            split_ref[source], w_ref[plan_ref[plan.near_t + k]], dims
        )


def near_kernel(plan, forward, plan_ref, w_ref, split_ref, sum_ref):
    near_products(plan, plan_ref, w_ref, split_ref, sum_ref, forward)


def backed_up(
    plan, reach, width, plan_ref, w_ref, part_ref, parts, all_ref, ext_ref, sum_ref
):
    rows = part_ref.shape[1]
    me = lax.axis_index("dom")
    collect(all_ref, parts)
    for o, f in enumerate(offsets(reach)):
        at = place(me, f)
        for m in range(width):
            store_split(ext_ref, o * width + m, all_ref[at, m * rows : (m + 1) * rows])
    for k in range(plan.blocks):
        sum_ref[k] = part_ref[k]
    count = plan_ref[plan.far]
    for k in range(plan.slots):
        slot = plan_ref[plan.far_c + k] - plan.blocks
        into = jnp.where(k < count, plan_ref[plan.far_r + k], plan.blocks)
        sum_ref[into] = sum_ref[into] + product(
            ext_ref[slot], w_ref[plan_ref[plan.far_t + k]], NT
        )


def goal_of(plan, plan_ref, rows, lanes):
    row = lax.broadcasted_iota(jnp.int32, (rows, lanes), 0)
    dest = jnp.zeros((rows, lanes), jnp.int32)
    for d in range(rows):
        dest = jnp.where(row == d, plan_ref[plan.dest + d], dest)
    return dest


def with_goal(k, blocks, growth_ref, sum_ref, dest, me):
    _, rows, lanes = sum_ref.shape
    node = (me * blocks + k) * lanes + lax.broadcasted_iota(jnp.int32, (rows, lanes), 1)
    return growth_ref[k] * sum_ref[k] + jnp.where(node == dest, GOAL_GAIN, 0.0)


def backup_kernel(
    plan, reach, width, plan_ref, w_ref, part_ref, growth_ref,
    got1, got2, got3, got4, got5,
    z_ref, next_ref, pairs_ref, ends_ref, all_ref, ext_ref, sum_ref,
):
    blocks, rows, lanes = z_ref.shape
    me = lax.axis_index("dom")
    backed_up(
        plan, reach, width, plan_ref, w_ref, part_ref,
        (got1, got2, got3, got4, got5), all_ref, ext_ref, sum_ref,
    )
    dest = goal_of(plan, plan_ref, rows, lanes)
    for k in range(blocks):
        z = with_goal(k, blocks, growth_ref, sum_ref, dest, me)
        z_ref[k] = z
        store_split(next_ref, k, z)
    send_items(
        pairs_ref, ends_ref, reach, 1,
        send_slots(width, lambda o, m: z_ref[plan_ref[plan.send + o * width + m]]),
    )


def far_flows(plan, plan_ref, w_ref, split_ref, flow_ref):
    for k in range(plan.slots + 1):
        flow_ref[k] = jnp.zeros(flow_ref.shape[1:], jnp.float32)
    count = plan_ref[plan.far]
    for k in range(plan.slots):
        slot = plan_ref[plan.far_c + k] - plan.blocks
        into = jnp.where(k < count, slot, plan.slots)
        flow_ref[into] = flow_ref[into] + product(
            split_ref[plan_ref[plan.far_r + k]], w_ref[plan_ref[plan.far_t + k]], NN
        )


def turn_kernel(
    plan, reach, width, plan_ref, w_ref, part_ref, growth_ref,
    got1, got2, got3, got4, got5, start_ref,
    z_ref, next_ref, pairs_ref, ends_ref, all_ref, ext_ref, sum_ref, flow_ref,
):
    blocks = plan.blocks
    _, rows, lanes = part_ref.shape
    me = lax.axis_index("dom")
    backed_up(
        plan, reach, width, plan_ref, w_ref, part_ref,
        (got1, got2, got3, got4, got5), all_ref, ext_ref, sum_ref,
    )
    dest = goal_of(plan, plan_ref, rows, lanes)
    for k in range(blocks):
        z = with_goal(k, blocks, growth_ref, sum_ref, dest, me)
        span = slice(k * lanes, (k + 1) * lanes)
        z_ref[k] = z
        store_split(next_ref, k, growth_ref[k] * start_ref[:, span].astype(jnp.float32) / z)
    far_flows(plan, plan_ref, w_ref, next_ref, flow_ref)
    send_items(
        pairs_ref, ends_ref, reach, -1, send_slots(width, lambda o, m: flow_ref[o * width + m])
    )


def flows(
    plan, count, reach, width, plan_ref, w_ref, growth_ref, sum_ref, parts,
    u_ref, next_ref, all_ref, flow_ref,
):
    blocks, rows, _ = u_ref.shape
    me = lax.axis_index("dom")
    for k in range(blocks):
        u_ref[k] = sum_ref[k]
    collect(all_ref, parts)
    for o, f in enumerate(offsets(reach)):
        there = present(me, count, f)
        at = place(me, -f)
        for m in range(width):
            b = plan_ref[plan.send + o * width + m]
            piece = all_ref[at, m * rows : (m + 1) * rows]
            u_ref[b] = u_ref[b] + jnp.where(there, piece, 0.0)
    for k in range(blocks):
        store_split(next_ref, k, growth_ref[k] * u_ref[k])
    far_flows(plan, plan_ref, w_ref, next_ref, flow_ref)


def spread_kernel(
    plan, count, reach, width, plan_ref, w_ref, growth_ref, sum_ref,
    got1, got2, got3, got4, got5,
    u_ref, next_ref, pairs_ref, ends_ref, all_ref, flow_ref,
):
    flows(
        plan, count, reach, width, plan_ref, w_ref, growth_ref, sum_ref,
        (got1, got2, got3, got4, got5), u_ref, next_ref, all_ref, flow_ref,
    )
    send_items(
        pairs_ref, ends_ref, reach, -1, send_slots(width, lambda o, m: flow_ref[o * width + m])
    )


def last_kernel(
    plan, count, reach, width, plan_ref, w_ref, growth_ref, sum_ref,
    got1, got2, got3, got4, got5, z1_got, z2_got, z3_got, z4_got, z5_got,
    u_ref, next_ref, pairs_ref, ends_ref, all_ref, flow_ref, far_ref,
):
    rows = u_ref.shape[1]
    me = lax.axis_index("dom")
    flows(
        plan, count, reach, width, plan_ref, w_ref, growth_ref, sum_ref,
        (got1, got2, got3, got4, got5), u_ref, next_ref, all_ref, flow_ref,
    )
    collect(far_ref, (z1_got, z2_got, z3_got, z4_got, z5_got))
    row = lax.broadcasted_iota(jnp.int32, ends_ref.shape[1:], 0)

    def item(o, ref, where):
        at = place(me, offset_of(o, reach))
        sums = jnp.zeros(ends_ref.shape[1:], jnp.float32)
        for m in range(width):
            lost = far_ref[at, m * rows : (m + 1) * rows] * flow_ref[o * width + m]
            sums = jnp.where(row == m, jnp.sum(lost, axis=0, keepdims=True), sums)
        ref[where] = sums

    send_items(pairs_ref, ends_ref, reach, -1, item)


def node_kernel(
    plan, plan_ref, w_ref, split_ref, z0_ref, z1_ref, z2_ref, u1_ref, u2_ref, visit_ref,
    node_ref, sum_ref,
):
    blocks, _, lanes = z0_ref.shape
    near_products(plan, plan_ref, w_ref, split_ref, sum_ref, False)
    for k in range(blocks):
        left = (
            visit_ref[:, k * lanes : (k + 1) * lanes].astype(jnp.float32)
            - z2_ref[k] * u1_ref[k]
            - z1_ref[k] * u2_ref[k]
            - z0_ref[k] * sum_ref[k]
        )
        node_ref[k] = jnp.sum(left, axis=0, keepdims=True)


def gradient_kernel(
    plan, count, reach, width, scale, plan_ref, v_ref, f_ref, act_ref, node_ref,
    got1, got2, got3, got4, got5, packed_ref, total_ref, all_ref,
):
    blocks, _, lanes = node_ref.shape
    me = lax.axis_index("dom")
    collect(all_ref, (got1, got2, got3, got4, got5))
    for k in range(blocks):
        total_ref[k] = node_ref[k]
    for o, f in enumerate(offsets(reach)):
        there = present(me, count, f)
        at = place(me, -f)
        for m in range(width):
            b = plan_ref[plan.send + o * width + m]
            total_ref[b] = total_ref[b] - jnp.where(there, all_ref[at, m : m + 1], 0.0)
    hidden = act_ref.shape[0]
    out_sum = jnp.zeros((hidden, lanes), jnp.float32)
    bias_sum = jnp.zeros((hidden, lanes), jnp.float32)
    grad = jnp.zeros((hidden, f_ref.shape[1]), jnp.float32)
    group = 4
    for c in range(blocks // group):
        highs = []
        lows = []
        for k in range(c * group, (c + 1) * group):
            act = act_ref[:, k * lanes : (k + 1) * lanes]
            node = total_ref[k] * scale
            weighted = act * node
            pre = node - weighted * act
            out_sum = out_sum + weighted
            bias_sum = bias_sum + pre
            high = pre.astype(jnp.bfloat16)
            highs.append(high)
            lows.append((pre - high.astype(jnp.float32)).astype(jnp.bfloat16))
        f = f_ref[c * group * lanes : (c + 1) * group * lanes]
        grad = grad + lax.dot_general(
            jnp.concatenate(highs, axis=1), f, NN, preferred_element_type=jnp.float32
        )
        grad = grad + lax.dot_general(
            jnp.concatenate(lows, axis=1), f, NN, preferred_element_type=jnp.float32
        )
    v = v_ref[...]
    core = me & 1
    half = packed_ref.shape[1]
    parts = hidden // lanes
    tall = hidden * f_ref.shape[1] // lanes

    def put(at, rows):
        packed_ref[jnp.bitwise_xor(core, at // half), at % half : at % half + rows.shape[0]] = rows

    for j in range(parts):
        span = slice(j * lanes, (j + 1) * lanes)
        turned = grad[span].T * v[:, span]
        for i in range(f_ref.shape[1] // 8):
            put((i * parts + j) * 8, turned[i * 8 : (i + 1) * 8])
    ones = jnp.ones((8, lanes), jnp.float32)
    across = lambda x: lax.dot_general(
        ones, x, NT, precision=lax.Precision.HIGHEST, preferred_element_type=jnp.float32
    )[:1]
    bias, out = across(bias_sum) * v, across(out_sum)
    cut = lambda x: [x[:, j * lanes : (j + 1) * lanes] for j in range(parts)]
    put(tall, jnp.concatenate(cut(bias) + cut(out), axis=0))
    for at in range(tall + 2 * parts, 2 * half, 8):
        put(at, jnp.zeros((8, lanes), jnp.float32))


def finish_kernel(mine_ref, other_ref, grad_hbm, bias_hbm, out_hbm, both_ref, bias_ref, out_ref, sem):
    half = mine_ref.shape[0]
    tall, parts = grad_hbm.shape[0], bias_hbm.shape[0]
    core = lax.axis_index("dom") & 1
    both_ref[core] = mine_ref[...]
    both_ref[1 - core] = other_ref[...]
    which, at = tall // half, tall % half
    bias_ref[...] = both_ref[which, at : at + parts]
    out_ref[...] = both_ref[which, at + parts : at + 2 * parts]
    pieces = [(bias_ref, bias_hbm), (out_ref, out_hbm)]
    for h in range(2):
        start, stop = h * half, min((h + 1) * half, tall)
        if start < stop:
            pieces.append((both_ref.at[h, : stop - start], grad_hbm.at[start:stop]))
    copies = [pltpu.make_async_copy(src, dst, sem.at[k]) for k, (src, dst) in enumerate(pieces)]
    for copy in copies:
        copy.start()
    for copy in copies:
        copy.wait()


def values_kernel(z_ref, values_ref):
    blocks, _, lanes = z_ref.shape
    for k in range(blocks):
        values_ref[:, k * lanes : (k + 1) * lanes] = jnp.log(z_ref[k])


def local(
    features, w_input, b_input, w_output, terminal, start_counts, visit_counts, dest_nodes,
    tile_rows, tile_cols, send_blocks, tile_weight,
):
    f32, bf16 = jnp.float32, jnp.bfloat16
    nodes, feat = features.shape
    tiles, lanes, _ = tile_weight.shape
    blocks = nodes // lanes
    rows = terminal.shape[0]
    hidden = w_input.shape[1]
    reach = send_blocks.shape[0] // 2
    width = send_blocks.shape[1]
    slots = 2 * reach * width
    count = lax.axis_size("dom")
    assert reach == 4 and count % 8 == 0
    shape = lambda *s: jax.ShapeDtypeStruct(s, f32)
    row_v = w_output[None, :]

    plan = Plan(blocks, tiles, slots, rows)
    like = lambda x: jax.ShapeDtypeStruct(x.shape, x.dtype)
    field = shape(blocks, rows, lanes)
    padded = shape(blocks + 1, rows, lanes)
    halves = jax.ShapeDtypeStruct((blocks, 2 * rows, lanes), bf16)
    parcels = (shape(3, 2, width * rows, lanes), shape(2, width * rows, lanes))
    smalls = (shape(3, 2, 8, lanes), shape(2, 8, lanes))
    all_s = pltpu.VMEM((PLACES, width * rows, lanes), f32)
    ext_s = pltpu.VMEM((slots, 2 * rows, lanes), bf16)
    sum_s = pltpu.VMEM((blocks + 1, rows, lanes), f32)
    flow_s = pltpu.VMEM((slots + 1, rows, lanes), f32)
    bind = lambda kernel, *lead: functools.partial(kernel, *lead, reach, width)
    flops = 2 * tiles * lanes * lanes * 2 * rows
    moved = tiles * lanes * lanes * 2
    send_t = send_blocks.T
    row_b = b_input[None, :]

    z0, split, pairs, ends = call(
        bind(first_kernel),
        (field, halves, *parcels),
        [
            pltpu.SMEM(send_t.shape, jnp.int32),
            pltpu.VMEM(terminal.shape, f32),
            pltpu.SemaphoreType.DMA((4,)),
            pltpu.SemaphoreType.DMA,
        ],
        (),
        (),
        flops,
        moved,
        hbm=(send_t, terminal),
    )

    def load():
        return call(
            functools.partial(load_kernel, plan),
            (
                jax.ShapeDtypeStruct((plan.size, lanes), jnp.int32),
                *map(like, (tile_weight, features, w_input, row_b, row_v)),
            ),
            [
                pltpu.SMEM((plan.size,), jnp.int32),
                pltpu.SMEM(tile_rows.shape, jnp.int32),
                pltpu.SMEM(tile_cols.shape, jnp.int32),
                pltpu.SMEM(send_t.shape, jnp.int32),
                pltpu.SMEM(dest_nodes.shape, jnp.int32),
                pltpu.SemaphoreType.DMA((5,)),
                pltpu.SemaphoreType.DMA((4,)),
            ],
            (),
            (),
            flops,
            moved,
            hbm=(tile_rows, tile_cols, send_t, dest_nodes, tile_weight, features, w_input, row_b, row_v),
            after=(ends,),
        )

    far, (plans, weight, feature, w_in, b_in, v_out) = exchange(pairs, ends, load)

    def near(split, forward):
        kernel = functools.partial(near_kernel, plan, forward)
        return call(kernel, padded, [], (plans,), (weight, split), flops, moved)

    act, growth = call(
        network_kernel,
        (shape(hidden, nodes), shape(blocks, 1, lanes)),
        [],
        (),
        (w_in, b_in, v_out, feature),
        2 * nodes * hidden * feat,
        nodes * hidden * 4,
    )

    def backup(part, got):
        return call(
            bind(backup_kernel, plan),
            (field, halves, *parcels),
            [all_s, ext_s, sum_s],
            (plans,),
            (weight, part, growth, *got),
            flops,
            moved,
        )

    z1, split, pairs, ends = backup(near(split, True), far)
    got, part = exchange(pairs, ends, lambda: near(split, True))
    z2, split2, pairs, ends = backup(part, got)
    got, part = exchange(pairs, ends, lambda: near(split2, True))
    z3, split3, pairs, ends = call(
        bind(turn_kernel, plan),
        (field, halves, *parcels),
        [all_s, ext_s, sum_s, flow_s],
        (plans,),
        (weight, part, growth, *got, start_counts),
        2 * flops,
        moved,
    )
    values = call(values_kernel, shape(rows, nodes), [], (), (z3,), flops // 8, nodes * rows * 8)
    got, part = exchange(pairs, ends, lambda: near(split3, False))
    u1, split4, pairs, ends = call(
        bind(spread_kernel, plan, count),
        (field, halves, *parcels),
        [all_s, flow_s],
        (plans,),
        (weight, growth, part, *got),
        flops,
        moved,
    )
    got, part = exchange(pairs, ends, lambda: near(split4, False))
    u2, split5, pairs, ends = call(
        bind(last_kernel, plan, count),
        (field, halves, *smalls),
        [all_s, flow_s, all_s],
        (plans,),
        (weight, growth, part, *got, *far),
        flops,
        moved,
    )
    got, node = exchange(
        pairs,
        ends,
        lambda: call(
            functools.partial(node_kernel, plan),
            shape(blocks, 1, lanes),
            [sum_s],
            (plans,),
            (weight, split5, z0, z1, z2, u1, u2, visit_counts),
            flops,
            moved,
        ),
    )
    every = ("dest", "dom")
    members = count * lax.axis_size("dest")
    tall = hidden * feat // lanes
    share = -(-(tall + 2 * hidden // lanes) // members)
    half = share * members // 2
    scale = 1.0 / math.sqrt(nodes * count * rows * lax.axis_size("dest"))
    packed = call(
        functools.partial(gradient_kernel, plan, count, reach, width, scale),
        shape(2, half, lanes),
        [
            pltpu.VMEM((blocks, 1, lanes), f32),
            pltpu.VMEM((PLACES, 8, lanes), f32),
        ],
        (plans,),
        (v_out, feature, act, node, *got),
        4 * nodes * hidden * feat,
        nodes * hidden * 4,
    )
    twins = [(i, i ^ 1) for i in range(count)]
    mine = packed[0] + lax.ppermute(packed[1], "dom", twins)
    same_core = [[i for i in range(members) if i % 2 == core] for core in range(2)]
    swap = lambda x: lax.all_to_all(x, every, 0, 0, tiled=True, axis_index_groups=same_core)
    mine = mine.reshape(members // 2, 1, share * lanes)
    mine = jnp.broadcast_to(swap(mine).sum(axis=0, keepdims=True), mine.shape)
    mine = swap(mine).reshape(half, lanes)
    other = lax.ppermute(mine, "dom", twins)
    in_hbm = pl.BlockSpec(memory_space=pltpu.HBM)
    in_vmem = pl.BlockSpec(memory_space=pltpu.VMEM)
    parts = hidden // lanes
    grad, bias, out = pl.pallas_call(
        finish_kernel,
        out_shape=(shape(tall, lanes), shape(parts, lanes), shape(parts, lanes)),
        in_specs=[in_vmem] * 2,
        out_specs=[in_hbm] * 3,
        scratch_shapes=[
            pltpu.VMEM((2, half, lanes), f32),
            pltpu.VMEM((parts, lanes), f32),
            pltpu.VMEM((parts, lanes), f32),
            pltpu.SemaphoreType.DMA((4,)),
        ],
        compiler_params=pltpu.CompilerParams(vmem_limit_bytes=VMEM_GRANT),
    )(mine, other)
    grad = grad.reshape(feat // 8, parts, 8, lanes).transpose(0, 2, 1, 3).reshape(feat, hidden)
    return values, grad, bias.reshape(-1), out.reshape(-1)


def solution(mesh):
    in_specs = (
        P("dom", None),
        P(),
        P(),
        P(),
        P("dest", "dom"),
        P("dest", "dom"),
        P("dest", "dom"),
        P("dest"),
        P("dom"),
        P("dom"),
        P("dom", None),
        P("dom", None, None),
    )
    out_specs = (P("dest", "dom"), P(), P(), P())
    return jax.shard_map(local, mesh=mesh, in_specs=in_specs, out_specs=out_specs, check_vma=False)
```

```python
import functools
import math

import jax
import jax.numpy as jnp
from jax import lax
from jax.experimental import pallas as pl
from jax.experimental.pallas import tpu as pltpu
from jax.sharding import PartitionSpec as P

STEPS = 3
GOAL_GAIN = 32.0
VMEM_GRANT = 20 << 20

HOLD = lambda x: pltpu.with_memory_space_constraint(x, pltpu.HBM)
NT = (((1,), (1,)), ((), ()))
NN = (((1,), (0,)), ((), ()))


def offset_of(o, reach):
    return o - reach if o < reach else o - reach + 1


def present(me, count, shift):
    there = me + shift
    return jnp.logical_and(there >= 0, there < count)


def place(me, shift):
    origin = me - shift
    k = jnp.bitwise_xor(origin, me) & 3
    odd = (me >> 2) & 1
    apart = (origin >> 2) - (me >> 2)
    here = 2 * (k - 1) + (1 if shift > 0 else 0)
    below = jnp.where(odd == 1, 6, 10) + k
    above = jnp.where(odd == 1, 10, 6) + k
    return jnp.where(apart == 0, here, jnp.where(apart < 0, below, above))


PLACES = 14


def exchange(pairs, ends, work):
    me = lax.axis_index("dom")
    devices = range(lax.axis_size("dom"))
    group_even = (me // 4) % 2 == 0

    def partner(i):
        j = (i // 4 + (1 if (i // 4) % 2 == 1 else -1)) * 4 + i % 4
        return j if j in devices else i ^ 1

    flip = lambda x, bits: lax.ppermute(x, "dom", [(i, i ^ bits) for i in devices])
    near = [flip(pairs[k - 1], k) for k in (1, 2, 3)]
    near, done = lax.optimization_barrier((near, work()))
    up = jnp.stack([ends[1], *(x[1] for x in near)])
    down = jnp.stack([ends[0], *(x[0] for x in near)])
    first = flip(jnp.where(group_even, up, down), 4)
    second = lax.ppermute(
        jnp.where(group_even, down, up), "dom", [(i, partner(i)) for i in devices]
    )
    return (*near, first, second), done


class Column:
    def __init__(self, ref):
        self.ref = ref

    def __getitem__(self, k):
        return self.ref[k, 0]


def call(kernel, out_shape, scratch, plans, vmem, flops, moved, hbm=(), after=()):
    space = lambda kind: pl.BlockSpec(memory_space=kind)
    out_specs = jax.tree.map(lambda _: space(pltpu.VMEM), out_shape)
    inner, at, lead = kernel, len(hbm), len(hbm) + len(plans)
    stop, span = lead + len(vmem), len(after)

    def kernel(*refs):
        columns = [Column(ref) for ref in refs[at:lead]]
        inner(*refs[:at], *columns, *refs[lead:stop], *refs[stop + span :])

    hbm = [HOLD(x) for x in hbm]
    return pl.pallas_call(
        kernel,
        out_shape=out_shape,
        in_specs=[space(pltpu.HBM)] * len(hbm)
        + [space(pltpu.VMEM)] * (len(plans) + len(vmem))
        + [space(pl.ANY)] * len(after),
        out_specs=out_specs,
        scratch_shapes=scratch,
        compiler_params=pltpu.CompilerParams(vmem_limit_bytes=VMEM_GRANT),
        cost_estimate=pl.CostEstimate(flops=flops, bytes_accessed=moved, transcendentals=0),
    )(*hbm, *plans, *vmem, *after)


def store_split(ref, k, x):
    rows = x.shape[0]
    high = x.astype(jnp.bfloat16)
    low = (x - high.astype(jnp.float32)).astype(jnp.bfloat16)
    ref[k, :rows] = high
    ref[k, rows:] = low


def product(lhs, rhs, dims):
    both = lax.dot_general(lhs, rhs, dims, preferred_element_type=jnp.float32)
    rows = both.shape[0] // 2
    return both[:rows] + both[rows:]


def offsets(reach):
    return [offset_of(o, reach) for o in range(2 * reach)]


def send_items(pairs, ends_ref, reach, sign, item):
    core = lax.axis_index("dom") & 1
    for o, f in enumerate(offsets(reach)):
        shift = sign * f
        side = 1 if shift > 0 else 0
        if abs(shift) == reach:
            item(o, ends_ref, (side,))
        elif shift % 2 == 0:
            item(o, pairs, (1, side))
        else:
            first = shift in (-3, 1)
            item(o, pairs, (2 * core if first else 2 - 2 * core, side))


def send_slots(width, source):
    def item(o, ref, at):
        for m in range(width):
            piece = source(o, m)
            rows = piece.shape[0]
            ref[(*at, slice(m * rows, (m + 1) * rows))] = piece

    return item


def collect(all_ref, parts):
    at = 0
    for part in parts:
        for k in range(part.shape[0]):
            all_ref[at] = part[k]
            at += 1


class Plan:
    def __init__(self, blocks, tiles, slots, rows):
        at = 0
        for name, size in (
            ("far_t", slots), ("far_r", slots), ("far_c", slots),
            ("near_t", tiles - blocks), ("near_r", tiles - blocks), ("near_c", tiles - blocks),
            ("send", slots), ("dest", rows), ("near", 1), ("far", 1),
        ):
            setattr(self, name, at)
            at += size
        self.size = at
        self.blocks, self.slots, self.extra = blocks, slots, tiles - blocks


def load_kernel(
    plan, rows_hbm, cols_hbm, send_hbm, dest_hbm, tile_hbm, f_hbm, w_hbm, b_hbm, v_hbm,
    table_ref, tile_ref, f_ref, w_ref, b_ref, v_ref,
    plan_ref, rows_ref, cols_ref, send_ref, dest_ref, sem, small,
):
    smalls = [
        pltpu.make_async_copy(src, dst, small.at[k])
        for k, (src, dst) in enumerate(
            ((rows_hbm, rows_ref), (cols_hbm, cols_ref), (send_hbm, send_ref), (dest_hbm, dest_ref))
        )
    ]
    larges = [
        pltpu.make_async_copy(src, dst, sem.at[k])
        for k, (src, dst) in enumerate(
            ((f_hbm, f_ref), (w_hbm, w_ref), (b_hbm, b_ref), (v_hbm, v_ref), (tile_hbm, tile_ref))
        )
    ]
    for copy in smalls + larges:
        copy.start()
    for copy in smalls:
        copy.wait()
    for k in range(plan.size):
        plan_ref[k] = 0
    width = send_ref.shape[0]
    for k in range(plan.slots):
        plan_ref[plan.far_c + k] = plan.blocks
        plan_ref[plan.send + k] = send_ref[k % width, k // width]
    for k in range(dest_ref.shape[0]):
        plan_ref[plan.dest + k] = dest_ref[k]

    def sort_tile(k, counts):
        near, far = counts
        t = plan.blocks + k
        r, c = rows_ref[t], cols_ref[t]
        apart = c >= plan.blocks
        at = jnp.where(apart, plan.far_t + far, plan.near_t + near)
        step = jnp.where(apart, plan.slots, plan.extra)
        plan_ref[at] = t
        plan_ref[at + step] = r
        plan_ref[at + 2 * step] = c
        one = apart.astype(jnp.int32)
        return near + 1 - one, far + one

    near, far = lax.fori_loop(0, plan.extra, sort_tile, (jnp.int32(0), jnp.int32(0)))
    plan_ref[plan.near] = near
    plan_ref[plan.far] = far
    for k in range(plan.size):
        table_ref[k : k + 1] = jnp.full((1, table_ref.shape[1]), plan_ref[k], jnp.int32)
    for copy in larges:
        copy.wait()


def network_kernel(w_ref, b_ref, v_ref, f_ref, act_ref, growth_ref):
    lanes = growth_ref.shape[2]
    hidden = act_ref.shape[0]
    group = 2
    w = w_ref[...].T
    b = jnp.broadcast_to(b_ref[...], (lanes, hidden)).T
    v = jnp.broadcast_to(v_ref[...], (lanes, hidden)).T
    for c in range(growth_ref.shape[0] // group):
        f = f_ref[c * group * lanes : (c + 1) * group * lanes]
        pre = lax.dot_general(w, f, NT, preferred_element_type=jnp.float32)
        for k in range(group):
            at = c * group + k
            act = jnp.tanh(pre[:, k * lanes : (k + 1) * lanes] + b)
            act_ref[:, at * lanes : (at + 1) * lanes] = act
            growth_ref[at] = jnp.exp(jnp.sum(act * v, axis=0, keepdims=True))


def first_kernel(
    reach, width, send_hbm, term_hbm, z_ref, split_ref, pairs_ref, ends_ref, send_ref, term_ref, sem, small
):
    blocks, _, lanes = z_ref.shape
    parts = sem.shape[0]
    span = blocks // parts
    asked = pltpu.make_async_copy(send_hbm, send_ref, small)
    cut = lambda ref, i: ref.at[:, i * span * lanes : (i + 1) * span * lanes]
    copies = [
        pltpu.make_async_copy(cut(term_hbm, i), cut(term_ref, i), sem.at[i]) for i in range(parts)
    ]
    asked.start()
    for copy in copies:
        copy.start()
    for i, copy in enumerate(copies):
        copy.wait()
        for k in range(i * span, (i + 1) * span):
            z = jnp.exp(term_ref[:, k * lanes : (k + 1) * lanes])
            z_ref[k] = z
            store_split(split_ref, k, z)
    asked.wait()
    send_items(
        pairs_ref, ends_ref, reach, 1, send_slots(width, lambda o, m: z_ref[send_ref[m, o]])
    )


def near_products(plan, plan_ref, w_ref, split_ref, sum_ref, forward):
    dims = NT if forward else NN
    for k in range(plan.blocks):
        sum_ref[k] = product(split_ref[k], w_ref[k], dims)
    count = plan_ref[plan.near]
    for k in range(plan.extra):
        r, c = plan_ref[plan.near_r + k], plan_ref[plan.near_c + k]
        source, into = (c, r) if forward else (r, c)
        into = jnp.where(k < count, into, plan.blocks)
        sum_ref[into] = sum_ref[into] + product(
            split_ref[source], w_ref[plan_ref[plan.near_t + k]], dims
        )


def near_kernel(plan, forward, plan_ref, w_ref, split_ref, sum_ref):
    near_products(plan, plan_ref, w_ref, split_ref, sum_ref, forward)


def backed_up(
    plan, reach, width, plan_ref, w_ref, part_ref, parts, all_ref, ext_ref, sum_ref
):
    rows = part_ref.shape[1]
    me = lax.axis_index("dom")
    collect(all_ref, parts)
    for o, f in enumerate(offsets(reach)):
        at = place(me, f)
        for m in range(width):
            store_split(ext_ref, o * width + m, all_ref[at, m * rows : (m + 1) * rows])
    for k in range(plan.blocks):
        sum_ref[k] = part_ref[k]
    count = plan_ref[plan.far]
    for k in range(plan.slots):
        slot = plan_ref[plan.far_c + k] - plan.blocks
        into = jnp.where(k < count, plan_ref[plan.far_r + k], plan.blocks)
        sum_ref[into] = sum_ref[into] + product(
            ext_ref[slot], w_ref[plan_ref[plan.far_t + k]], NT
        )


def goal_of(plan, plan_ref, rows, lanes):
    row = lax.broadcasted_iota(jnp.int32, (rows, lanes), 0)
    dest = jnp.zeros((rows, lanes), jnp.int32)
    for d in range(rows):
        dest = jnp.where(row == d, plan_ref[plan.dest + d], dest)
    return dest


def with_goal(k, blocks, growth_ref, sum_ref, dest, me):
    _, rows, lanes = sum_ref.shape
    node = (me * blocks + k) * lanes + lax.broadcasted_iota(jnp.int32, (rows, lanes), 1)
    return growth_ref[k] * sum_ref[k] + jnp.where(node == dest, GOAL_GAIN, 0.0)


def backup_kernel(
    plan, reach, width, plan_ref, w_ref, part_ref, growth_ref,
    got1, got2, got3, got4, got5,
    z_ref, next_ref, pairs_ref, ends_ref, all_ref, ext_ref, sum_ref,
):
    blocks, rows, lanes = z_ref.shape
    me = lax.axis_index("dom")
    backed_up(
        plan, reach, width, plan_ref, w_ref, part_ref,
        (got1, got2, got3, got4, got5), all_ref, ext_ref, sum_ref,
    )
    dest = goal_of(plan, plan_ref, rows, lanes)
    for k in range(blocks):
        z = with_goal(k, blocks, growth_ref, sum_ref, dest, me)
        z_ref[k] = z
        store_split(next_ref, k, z)
    send_items(
        pairs_ref, ends_ref, reach, 1,
        send_slots(width, lambda o, m: z_ref[plan_ref[plan.send + o * width + m]]),
    )


def far_flows(plan, plan_ref, w_ref, split_ref, flow_ref):
    for k in range(plan.slots + 1):
        flow_ref[k] = jnp.zeros(flow_ref.shape[1:], jnp.float32)
    count = plan_ref[plan.far]
    for k in range(plan.slots):
        slot = plan_ref[plan.far_c + k] - plan.blocks
        into = jnp.where(k < count, slot, plan.slots)
        flow_ref[into] = flow_ref[into] + product(
            split_ref[plan_ref[plan.far_r + k]], w_ref[plan_ref[plan.far_t + k]], NN
        )


def turn_kernel(
    plan, reach, width, plan_ref, w_ref, part_ref, growth_ref,
    got1, got2, got3, got4, got5, start_ref,
    z_ref, next_ref, pairs_ref, ends_ref, all_ref, ext_ref, sum_ref, flow_ref,
):
    blocks = plan.blocks
    _, rows, lanes = part_ref.shape
    me = lax.axis_index("dom")
    backed_up(
        plan, reach, width, plan_ref, w_ref, part_ref,
        (got1, got2, got3, got4, got5), all_ref, ext_ref, sum_ref,
    )
    dest = goal_of(plan, plan_ref, rows, lanes)
    for k in range(blocks):
        z = with_goal(k, blocks, growth_ref, sum_ref, dest, me)
        span = slice(k * lanes, (k + 1) * lanes)
        z_ref[k] = z
        store_split(next_ref, k, growth_ref[k] * start_ref[:, span].astype(jnp.float32) / z)
    far_flows(plan, plan_ref, w_ref, next_ref, flow_ref)
    send_items(
        pairs_ref, ends_ref, reach, -1, send_slots(width, lambda o, m: flow_ref[o * width + m])
    )


def flows(
    plan, count, reach, width, plan_ref, w_ref, growth_ref, sum_ref, parts,
    u_ref, next_ref, all_ref, flow_ref,
):
    blocks, rows, _ = u_ref.shape
    me = lax.axis_index("dom")
    for k in range(blocks):
        u_ref[k] = sum_ref[k]
    collect(all_ref, parts)
    for o, f in enumerate(offsets(reach)):
        there = present(me, count, f)
        at = place(me, -f)
        for m in range(width):
            b = plan_ref[plan.send + o * width + m]
            piece = all_ref[at, m * rows : (m + 1) * rows]
            u_ref[b] = u_ref[b] + jnp.where(there, piece, 0.0)
    for k in range(blocks):
        store_split(next_ref, k, growth_ref[k] * u_ref[k])
    far_flows(plan, plan_ref, w_ref, next_ref, flow_ref)


def spread_kernel(
    plan, count, reach, width, plan_ref, w_ref, growth_ref, sum_ref,
    got1, got2, got3, got4, got5,
    u_ref, next_ref, pairs_ref, ends_ref, all_ref, flow_ref,
):
    flows(
        plan, count, reach, width, plan_ref, w_ref, growth_ref, sum_ref,
        (got1, got2, got3, got4, got5), u_ref, next_ref, all_ref, flow_ref,
    )
    send_items(
        pairs_ref, ends_ref, reach, -1, send_slots(width, lambda o, m: flow_ref[o * width + m])
    )


def last_kernel(
    plan, count, reach, width, plan_ref, w_ref, growth_ref, sum_ref,
    got1, got2, got3, got4, got5, z1_got, z2_got, z3_got, z4_got, z5_got,
    u_ref, next_ref, pairs_ref, ends_ref, all_ref, flow_ref, far_ref,
):
    rows = u_ref.shape[1]
    me = lax.axis_index("dom")
    flows(
        plan, count, reach, width, plan_ref, w_ref, growth_ref, sum_ref,
        (got1, got2, got3, got4, got5), u_ref, next_ref, all_ref, flow_ref,
    )
    collect(far_ref, (z1_got, z2_got, z3_got, z4_got, z5_got))
    row = lax.broadcasted_iota(jnp.int32, ends_ref.shape[1:], 0)

    def item(o, ref, where):
        at = place(me, offset_of(o, reach))
        sums = jnp.zeros(ends_ref.shape[1:], jnp.float32)
        for m in range(width):
            lost = far_ref[at, m * rows : (m + 1) * rows] * flow_ref[o * width + m]
            sums = jnp.where(row == m, jnp.sum(lost, axis=0, keepdims=True), sums)
        ref[where] = sums

    send_items(pairs_ref, ends_ref, reach, -1, item)


def node_kernel(
    plan, plan_ref, w_ref, split_ref, z0_ref, z1_ref, z2_ref, u1_ref, u2_ref, visit_ref,
    node_ref, sum_ref,
):
    blocks, _, lanes = z0_ref.shape
    near_products(plan, plan_ref, w_ref, split_ref, sum_ref, False)
    for k in range(blocks):
        left = (
            visit_ref[:, k * lanes : (k + 1) * lanes].astype(jnp.float32)
            - z2_ref[k] * u1_ref[k]
            - z1_ref[k] * u2_ref[k]
            - z0_ref[k] * sum_ref[k]
        )
        node_ref[k] = jnp.sum(left, axis=0, keepdims=True)


def add_gradients(items, act_ref, f_ref, grad, out_sum, bias_sum):
    group = 4
    for c in range(0, len(items), group):
        highs = []
        lows = []
        for at, node in items[c : c + group]:
            act = act_ref[:, at]
            weighted = act * node
            pre = node - weighted * act
            out_sum = out_sum + weighted
            bias_sum = bias_sum + pre
            high = pre.astype(jnp.bfloat16)
            highs.append(high)
            lows.append((pre - high.astype(jnp.float32)).astype(jnp.bfloat16))
        f = jnp.concatenate([f_ref[at] for at, _ in items[c : c + group]], axis=0)
        grad = grad + lax.dot_general(
            jnp.concatenate(highs, axis=1), f, NN, preferred_element_type=jnp.float32
        )
        grad = grad + lax.dot_general(
            jnp.concatenate(lows, axis=1), f, NN, preferred_element_type=jnp.float32
        )
    return grad, out_sum, bias_sum


def own_gradient_kernel(scale, f_ref, act_ref, node_ref, grad_ref, out_ref, bias_ref):
    blocks, _, lanes = node_ref.shape
    items = [
        (slice(k * lanes, (k + 1) * lanes), node_ref[k] * scale) for k in range(blocks)
    ]
    zeros = [jnp.zeros(ref.shape, jnp.float32) for ref in (grad_ref, out_ref, bias_ref)]
    grad_ref[...], out_ref[...], bias_ref[...] = add_gradients(items, act_ref, f_ref, *zeros)


def gradient_kernel(
    plan, count, reach, width, scale, plan_ref, v_ref, f_ref, act_ref, grad_ref, out_ref, bias_ref,
    got1, got2, got3, got4, got5, packed_ref, all_ref,
):
    hidden, lanes = out_ref.shape
    me = lax.axis_index("dom")
    collect(all_ref, (got1, got2, got3, got4, got5))
    items = []
    for o, f in enumerate(offsets(reach)):
        there = present(me, count, f)
        at = place(me, -f)
        for m in range(width):
            block = plan_ref[plan.send + o * width + m]
            row = jnp.where(there, -scale * all_ref[at, m : m + 1], 0.0)
            items.append((pl.ds(pl.multiple_of(block * lanes, lanes), lanes), row))
    grad, out_sum, bias_sum = add_gradients(
        items, act_ref, f_ref, grad_ref[...], out_ref[...], bias_ref[...]
    )
    v = v_ref[...]
    core = me & 1
    half = packed_ref.shape[1]
    parts = hidden // lanes
    tall = hidden * f_ref.shape[1] // lanes

    def put(at, rows):
        packed_ref[jnp.bitwise_xor(core, at // half), at % half : at % half + rows.shape[0]] = rows

    for j in range(parts):
        span = slice(j * lanes, (j + 1) * lanes)
        turned = grad[span].T * v[:, span]
        for i in range(f_ref.shape[1] // 8):
            put((i * parts + j) * 8, turned[i * 8 : (i + 1) * 8])
    ones = jnp.ones((8, lanes), jnp.float32)
    across = lambda x: lax.dot_general(
        ones, x, NT, precision=lax.Precision.HIGHEST, preferred_element_type=jnp.float32
    )[:1]
    bias, out = across(bias_sum) * v, across(out_sum)
    cut = lambda x: [x[:, j * lanes : (j + 1) * lanes] for j in range(parts)]
    put(tall, jnp.concatenate(cut(bias) + cut(out), axis=0))
    for at in range(tall + 2 * parts, 2 * half, 8):
        put(at, jnp.zeros((8, lanes), jnp.float32))


def finish_kernel(mine_ref, other_ref, grad_hbm, bias_hbm, out_hbm, both_ref, bias_ref, out_ref, sem):
    half = mine_ref.shape[0]
    tall, parts = grad_hbm.shape[0], bias_hbm.shape[0]
    core = lax.axis_index("dom") & 1
    both_ref[core] = mine_ref[...]
    both_ref[1 - core] = other_ref[...]
    which, at = tall // half, tall % half
    bias_ref[...] = both_ref[which, at : at + parts]
    out_ref[...] = both_ref[which, at + parts : at + 2 * parts]
    pieces = [(bias_ref, bias_hbm), (out_ref, out_hbm)]
    for h in range(2):
        start, stop = h * half, min((h + 1) * half, tall)
        if start < stop:
            pieces.append((both_ref.at[h, : stop - start], grad_hbm.at[start:stop]))
    copies = [pltpu.make_async_copy(src, dst, sem.at[k]) for k, (src, dst) in enumerate(pieces)]
    for copy in copies:
        copy.start()
    for copy in copies:
        copy.wait()


def values_kernel(z_ref, values_ref):
    blocks, _, lanes = z_ref.shape
    for k in range(blocks):
        values_ref[:, k * lanes : (k + 1) * lanes] = jnp.log(z_ref[k])


def local(
    features, w_input, b_input, w_output, terminal, start_counts, visit_counts, dest_nodes,
    tile_rows, tile_cols, send_blocks, tile_weight,
):
    f32, bf16 = jnp.float32, jnp.bfloat16
    nodes, feat = features.shape
    tiles, lanes, _ = tile_weight.shape
    blocks = nodes // lanes
    rows = terminal.shape[0]
    hidden = w_input.shape[1]
    reach = send_blocks.shape[0] // 2
    width = send_blocks.shape[1]
    slots = 2 * reach * width
    count = lax.axis_size("dom")
    assert reach == 4 and count % 8 == 0
    shape = lambda *s: jax.ShapeDtypeStruct(s, f32)
    row_v = w_output[None, :]

    plan = Plan(blocks, tiles, slots, rows)
    like = lambda x: jax.ShapeDtypeStruct(x.shape, x.dtype)
    field = shape(blocks, rows, lanes)
    padded = shape(blocks + 1, rows, lanes)
    halves = jax.ShapeDtypeStruct((blocks, 2 * rows, lanes), bf16)
    parcels = (shape(3, 2, width * rows, lanes), shape(2, width * rows, lanes))
    smalls = (shape(3, 2, 8, lanes), shape(2, 8, lanes))
    all_s = pltpu.VMEM((PLACES, width * rows, lanes), f32)
    ext_s = pltpu.VMEM((slots, 2 * rows, lanes), bf16)
    sum_s = pltpu.VMEM((blocks + 1, rows, lanes), f32)
    flow_s = pltpu.VMEM((slots + 1, rows, lanes), f32)
    bind = lambda kernel, *lead: functools.partial(kernel, *lead, reach, width)
    flops = 2 * tiles * lanes * lanes * 2 * rows
    moved = tiles * lanes * lanes * 2
    send_t = send_blocks.T
    row_b = b_input[None, :]

    z0, split, pairs, ends = call(
        bind(first_kernel),
        (field, halves, *parcels),
        [
            pltpu.SMEM(send_t.shape, jnp.int32),
            pltpu.VMEM(terminal.shape, f32),
            pltpu.SemaphoreType.DMA((4,)),
            pltpu.SemaphoreType.DMA,
        ],
        (),
        (),
        flops,
        moved,
        hbm=(send_t, terminal),
    )

    def load():
        return call(
            functools.partial(load_kernel, plan),
            (
                jax.ShapeDtypeStruct((plan.size, lanes), jnp.int32),
                *map(like, (tile_weight, features, w_input, row_b, row_v)),
            ),
            [
                pltpu.SMEM((plan.size,), jnp.int32),
                pltpu.SMEM(tile_rows.shape, jnp.int32),
                pltpu.SMEM(tile_cols.shape, jnp.int32),
                pltpu.SMEM(send_t.shape, jnp.int32),
                pltpu.SMEM(dest_nodes.shape, jnp.int32),
                pltpu.SemaphoreType.DMA((5,)),
                pltpu.SemaphoreType.DMA((4,)),
            ],
            (),
            (),
            flops,
            moved,
            hbm=(tile_rows, tile_cols, send_t, dest_nodes, tile_weight, features, w_input, row_b, row_v),
            after=(ends,),
        )

    far, (plans, weight, feature, w_in, b_in, v_out) = exchange(pairs, ends, load)

    def near(split, forward):
        kernel = functools.partial(near_kernel, plan, forward)
        return call(kernel, padded, [], (plans,), (weight, split), flops, moved)

    act, growth = call(
        network_kernel,
        (shape(hidden, nodes), shape(blocks, 1, lanes)),
        [],
        (),
        (w_in, b_in, v_out, feature),
        2 * nodes * hidden * feat,
        nodes * hidden * 4,
    )

    def backup(part, got):
        return call(
            bind(backup_kernel, plan),
            (field, halves, *parcels),
            [all_s, ext_s, sum_s],
            (plans,),
            (weight, part, growth, *got),
            flops,
            moved,
        )

    z1, split, pairs, ends = backup(near(split, True), far)
    got, part = exchange(pairs, ends, lambda: near(split, True))
    z2, split2, pairs, ends = backup(part, got)
    got, part = exchange(pairs, ends, lambda: near(split2, True))
    z3, split3, pairs, ends = call(
        bind(turn_kernel, plan),
        (field, halves, *parcels),
        [all_s, ext_s, sum_s, flow_s],
        (plans,),
        (weight, part, growth, *got, start_counts),
        2 * flops,
        moved,
    )
    values = call(values_kernel, shape(rows, nodes), [], (), (z3,), flops // 8, nodes * rows * 8)
    got, part = exchange(pairs, ends, lambda: near(split3, False))
    u1, split4, pairs, ends = call(
        bind(spread_kernel, plan, count),
        (field, halves, *parcels),
        [all_s, flow_s],
        (plans,),
        (weight, growth, part, *got),
        flops,
        moved,
    )
    got, part = exchange(pairs, ends, lambda: near(split4, False))
    u2, split5, pairs, ends = call(
        bind(last_kernel, plan, count),
        (field, halves, *smalls),
        [all_s, flow_s, all_s],
        (plans,),
        (weight, growth, part, *got, *far),
        flops,
        moved,
    )
    got, node = exchange(
        pairs,
        ends,
        lambda: call(
            functools.partial(node_kernel, plan),
            shape(blocks, 1, lanes),
            [sum_s],
            (plans,),
            (weight, split5, z0, z1, z2, u1, u2, visit_counts),
            flops,
            moved,
        ),
    )
    every = ("dest", "dom")
    members = count * lax.axis_size("dest")
    tall = hidden * feat // lanes
    share = -(-(tall + 2 * hidden // lanes) // members)
    half = share * members // 2
    scale = 1.0 / math.sqrt(nodes * count * rows * lax.axis_size("dest"))
    own = call(
        functools.partial(own_gradient_kernel, scale),
        (shape(hidden, feat), shape(hidden, lanes), shape(hidden, lanes)),
        [],
        (),
        (feature, act, node),
        4 * nodes * hidden * feat,
        nodes * hidden * 4,
    )
    packed = call(
        functools.partial(gradient_kernel, plan, count, reach, width, scale),
        shape(2, half, lanes),
        [pltpu.VMEM((PLACES, 8, lanes), f32)],
        (plans,),
        (v_out, feature, act, *own, *got),
        4 * slots * lanes * hidden * feat,
        slots * lanes * hidden * 4,
    )
    twins = [(i, i ^ 1) for i in range(count)]
    mine = packed[0] + lax.ppermute(packed[1], "dom", twins)
    same_core = [[i for i in range(members) if i % 2 == core] for core in range(2)]
    swap = lambda x: lax.all_to_all(x, every, 0, 0, tiled=True, axis_index_groups=same_core)
    mine = mine.reshape(members // 2, 1, share * lanes)
    mine = jnp.broadcast_to(swap(mine).sum(axis=0, keepdims=True), mine.shape)
    mine = swap(mine).reshape(half, lanes)
    other = lax.ppermute(mine, "dom", twins)
    in_hbm = pl.BlockSpec(memory_space=pltpu.HBM)
    in_vmem = pl.BlockSpec(memory_space=pltpu.VMEM)
    parts = hidden // lanes
    grad, bias, out = pl.pallas_call(
        finish_kernel,
        out_shape=(shape(tall, lanes), shape(parts, lanes), shape(parts, lanes)),
        in_specs=[in_vmem] * 2,
        out_specs=[in_hbm] * 3,
        scratch_shapes=[
            pltpu.VMEM((2, half, lanes), f32),
            pltpu.VMEM((parts, lanes), f32),
            pltpu.VMEM((parts, lanes), f32),
            pltpu.SemaphoreType.DMA((4,)),
        ],
        compiler_params=pltpu.CompilerParams(vmem_limit_bytes=VMEM_GRANT),
    )(mine, other)
    grad = grad.reshape(feat // 8, parts, 8, lanes).transpose(0, 2, 1, 3).reshape(feat, hidden)
    return values, grad, bias.reshape(-1), out.reshape(-1)


def solution(mesh):
    in_specs = (
        P("dom", None),
        P(),
        P(),
        P(),
        P("dest", "dom"),
        P("dest", "dom"),
        P("dest", "dom"),
        P("dest"),
        P("dom"),
        P("dom"),
        P("dom", None),
        P("dom", None, None),
    )
    out_specs = (P("dest", "dom"), P(), P(), P())
    return jax.shard_map(local, mesh=mesh, in_specs=in_specs, out_specs=out_specs, check_vma=False)
```

```python
import functools
import math

import jax
import jax.numpy as jnp
from jax import lax
from jax.experimental import pallas as pl
from jax.experimental.pallas import tpu as pltpu
from jax.sharding import PartitionSpec as P

STEPS = 3
GOAL_GAIN = 32.0
VMEM_GRANT = 20 << 20

HOLD = lambda x: pltpu.with_memory_space_constraint(x, pltpu.HBM)
NT = (((1,), (1,)), ((), ()))
NN = (((1,), (0,)), ((), ()))


def offset_of(o, reach):
    return o - reach if o < reach else o - reach + 1


def present(me, count, shift):
    there = me + shift
    return jnp.logical_and(there >= 0, there < count)


def place(me, shift):
    origin = me - shift
    k = jnp.bitwise_xor(origin, me) & 3
    odd = (me >> 2) & 1
    apart = (origin >> 2) - (me >> 2)
    here = 2 * (k - 1) + (1 if shift > 0 else 0)
    below = jnp.where(odd == 1, 6, 10) + k
    above = jnp.where(odd == 1, 10, 6) + k
    return jnp.where(apart == 0, here, jnp.where(apart < 0, below, above))


PLACES = 14


def exchange(pairs, ends, work):
    me = lax.axis_index("dom")
    devices = range(lax.axis_size("dom"))
    group_even = (me // 4) % 2 == 0

    def partner(i):
        j = (i // 4 + (1 if (i // 4) % 2 == 1 else -1)) * 4 + i % 4
        return j if j in devices else i ^ 1

    flip = lambda x, bits: lax.ppermute(x, "dom", [(i, i ^ bits) for i in devices])
    near = [flip(pairs[k - 1], k) for k in (1, 2, 3)]
    near, done = lax.optimization_barrier((near, work()))
    up = jnp.stack([ends[1], *(x[1] for x in near)])
    down = jnp.stack([ends[0], *(x[0] for x in near)])
    first = flip(jnp.where(group_even, up, down), 4)
    second = lax.ppermute(
        jnp.where(group_even, down, up), "dom", [(i, partner(i)) for i in devices]
    )
    return (*near, first, second), done


class Column:
    def __init__(self, ref):
        self.ref = ref

    def __getitem__(self, k):
        return self.ref[k, 0]


def call(kernel, out_shape, scratch, plans, vmem, flops, moved, hbm=(), after=()):
    space = lambda kind: pl.BlockSpec(memory_space=kind)
    out_specs = jax.tree.map(lambda _: space(pltpu.VMEM), out_shape)
    inner, at, lead = kernel, len(hbm), len(hbm) + len(plans)
    stop, span = lead + len(vmem), len(after)

    def kernel(*refs):
        columns = [Column(ref) for ref in refs[at:lead]]
        inner(*refs[:at], *columns, *refs[lead:stop], *refs[stop + span :])

    hbm = [HOLD(x) for x in hbm]
    return pl.pallas_call(
        kernel,
        out_shape=out_shape,
        in_specs=[space(pltpu.HBM)] * len(hbm)
        + [space(pltpu.VMEM)] * (len(plans) + len(vmem))
        + [space(pl.ANY)] * len(after),
        out_specs=out_specs,
        scratch_shapes=scratch,
        compiler_params=pltpu.CompilerParams(vmem_limit_bytes=VMEM_GRANT),
        cost_estimate=pl.CostEstimate(flops=flops, bytes_accessed=moved, transcendentals=0),
    )(*hbm, *plans, *vmem, *after)


def store_split(ref, k, x):
    rows = x.shape[0]
    high = x.astype(jnp.bfloat16)
    low = (x - high.astype(jnp.float32)).astype(jnp.bfloat16)
    ref[k, :rows] = high
    ref[k, rows:] = low


def product(lhs, rhs, dims):
    both = lax.dot_general(lhs, rhs, dims, preferred_element_type=jnp.float32)
    rows = both.shape[0] // 2
    return both[:rows] + both[rows:]


def offsets(reach):
    return [offset_of(o, reach) for o in range(2 * reach)]


def send_items(pairs, ends_ref, reach, sign, item):
    core = lax.axis_index("dom") & 1
    for o, f in enumerate(offsets(reach)):
        shift = sign * f
        side = 1 if shift > 0 else 0
        if abs(shift) == reach:
            item(o, ends_ref, (side,))
        elif shift % 2 == 0:
            item(o, pairs, (1, side))
        else:
            first = shift in (-3, 1)
            item(o, pairs, (2 * core if first else 2 - 2 * core, side))


def send_slots(width, source):
    def item(o, ref, at):
        for m in range(width):
            piece = source(o, m)
            rows = piece.shape[0]
            ref[(*at, slice(m * rows, (m + 1) * rows))] = piece

    return item


def collect(all_ref, parts):
    at = 0
    for part in parts:
        for k in range(part.shape[0]):
            all_ref[at] = part[k]
            at += 1


class Plan:
    def __init__(self, blocks, tiles, slots, rows):
        at = 0
        for name, size in (
            ("far_t", slots), ("far_r", slots), ("far_c", slots),
            ("near_t", tiles - blocks), ("near_r", tiles - blocks), ("near_c", tiles - blocks),
            ("send", slots), ("dest", rows), ("near", 1), ("far", 1),
        ):
            setattr(self, name, at)
            at += size
        self.size = at
        self.blocks, self.slots, self.extra = blocks, slots, tiles - blocks


def load_kernel(
    plan, rows_hbm, cols_hbm, send_hbm, dest_hbm, tile_hbm, f_hbm, w_hbm, b_hbm, v_hbm,
    table_ref, tile_ref, f_ref, w_ref, b_ref, v_ref,
    plan_ref, rows_ref, cols_ref, send_ref, dest_ref, sem, small,
):
    smalls = [
        pltpu.make_async_copy(src, dst, small.at[k])
        for k, (src, dst) in enumerate(
            ((rows_hbm, rows_ref), (cols_hbm, cols_ref), (send_hbm, send_ref), (dest_hbm, dest_ref))
        )
    ]
    larges = [
        pltpu.make_async_copy(src, dst, sem.at[k])
        for k, (src, dst) in enumerate(
            ((f_hbm, f_ref), (w_hbm, w_ref), (b_hbm, b_ref), (v_hbm, v_ref), (tile_hbm, tile_ref))
        )
    ]
    for copy in smalls + larges:
        copy.start()
    for copy in smalls:
        copy.wait()
    for k in range(plan.size):
        plan_ref[k] = 0
    width = send_ref.shape[0]
    for k in range(plan.slots):
        plan_ref[plan.far_c + k] = plan.blocks
        plan_ref[plan.send + k] = send_ref[k % width, k // width]
    for k in range(dest_ref.shape[0]):
        plan_ref[plan.dest + k] = dest_ref[k]

    def sort_tile(k, counts):
        near, far = counts
        t = plan.blocks + k
        r, c = rows_ref[t], cols_ref[t]
        apart = c >= plan.blocks
        at = jnp.where(apart, plan.far_t + far, plan.near_t + near)
        step = jnp.where(apart, plan.slots, plan.extra)
        plan_ref[at] = t
        plan_ref[at + step] = r
        plan_ref[at + 2 * step] = c
        one = apart.astype(jnp.int32)
        return near + 1 - one, far + one

    near, far = lax.fori_loop(0, plan.extra, sort_tile, (jnp.int32(0), jnp.int32(0)))
    plan_ref[plan.near] = near
    plan_ref[plan.far] = far
    for k in range(plan.size):
        table_ref[k : k + 1] = jnp.full((1, table_ref.shape[1]), plan_ref[k], jnp.int32)
    for copy in larges:
        copy.wait()


def network_kernel(w_ref, b_ref, v_ref, f_ref, act_ref, growth_ref):
    lanes = growth_ref.shape[2]
    hidden = act_ref.shape[0]
    group = 2
    w = w_ref[...].T
    b = jnp.broadcast_to(b_ref[...], (lanes, hidden)).T
    v = jnp.broadcast_to(v_ref[...], (lanes, hidden)).T
    for c in range(growth_ref.shape[0] // group):
        f = f_ref[c * group * lanes : (c + 1) * group * lanes]
        pre = lax.dot_general(w, f, NT, preferred_element_type=jnp.float32)
        for k in range(group):
            at = c * group + k
            act = jnp.tanh(pre[:, k * lanes : (k + 1) * lanes] + b)
            act_ref[:, at * lanes : (at + 1) * lanes] = act
            growth_ref[at] = jnp.exp(jnp.sum(act * v, axis=0, keepdims=True))


def first_kernel(
    reach, width, send_hbm, term_hbm, z_ref, pairs_ref, ends_ref, send_ref, term_ref, sem, small
):
    blocks, _, lanes = z_ref.shape
    parts = sem.shape[0]
    span = blocks // parts
    asked = pltpu.make_async_copy(send_hbm, send_ref, small)
    cut = lambda ref, i: ref.at[:, i * span * lanes : (i + 1) * span * lanes]
    copies = [
        pltpu.make_async_copy(cut(term_hbm, i), cut(term_ref, i), sem.at[i]) for i in range(parts)
    ]
    asked.start()
    for copy in copies:
        copy.start()
    for i, copy in enumerate(copies):
        copy.wait()
        for k in range(i * span, (i + 1) * span):
            z_ref[k] = jnp.exp(term_ref[:, k * lanes : (k + 1) * lanes])
    asked.wait()
    send_items(
        pairs_ref, ends_ref, reach, 1, send_slots(width, lambda o, m: z_ref[send_ref[m, o]])
    )


def near_products(plan, plan_ref, w_ref, split_ref, sum_ref, forward):
    dims = NT if forward else NN
    for k in range(plan.blocks):
        sum_ref[k] = product(split_ref[k], w_ref[k], dims)
    count = plan_ref[plan.near]
    for k in range(plan.extra):
        r, c = plan_ref[plan.near_r + k], plan_ref[plan.near_c + k]
        source, into = (c, r) if forward else (r, c)
        into = jnp.where(k < count, into, plan.blocks)
        sum_ref[into] = sum_ref[into] + product(
            split_ref[source], w_ref[plan_ref[plan.near_t + k]], dims
        )


def near_kernel(plan, forward, plan_ref, w_ref, split_ref, sum_ref):
    near_products(plan, plan_ref, w_ref, split_ref, sum_ref, forward)


def near_values_kernel(plan, plan_ref, w_ref, z_ref, sum_ref, split_ref):
    for k in range(plan.blocks):
        store_split(split_ref, k, z_ref[k])
    near_products(plan, plan_ref, w_ref, split_ref, sum_ref, True)


def backed_up(
    plan, reach, width, plan_ref, w_ref, part_ref, parts, all_ref, ext_ref, sum_ref
):
    rows = part_ref.shape[1]
    me = lax.axis_index("dom")
    collect(all_ref, parts)
    for o, f in enumerate(offsets(reach)):
        at = place(me, f)
        for m in range(width):
            store_split(ext_ref, o * width + m, all_ref[at, m * rows : (m + 1) * rows])
    for k in range(plan.blocks):
        sum_ref[k] = part_ref[k]
    count = plan_ref[plan.far]
    for k in range(plan.slots):
        slot = plan_ref[plan.far_c + k] - plan.blocks
        into = jnp.where(k < count, plan_ref[plan.far_r + k], plan.blocks)
        sum_ref[into] = sum_ref[into] + product(
            ext_ref[slot], w_ref[plan_ref[plan.far_t + k]], NT
        )


def goal_of(plan, plan_ref, rows, lanes):
    row = lax.broadcasted_iota(jnp.int32, (rows, lanes), 0)
    dest = jnp.zeros((rows, lanes), jnp.int32)
    for d in range(rows):
        dest = jnp.where(row == d, plan_ref[plan.dest + d], dest)
    return dest


def with_goal(k, blocks, growth_ref, sum_ref, dest, me):
    _, rows, lanes = sum_ref.shape
    node = (me * blocks + k) * lanes + lax.broadcasted_iota(jnp.int32, (rows, lanes), 1)
    return growth_ref[k] * sum_ref[k] + jnp.where(node == dest, GOAL_GAIN, 0.0)


def backup_kernel(
    plan, reach, width, plan_ref, w_ref, part_ref, growth_ref,
    got1, got2, got3, got4, got5,
    z_ref, pairs_ref, ends_ref, all_ref, ext_ref, sum_ref,
):
    blocks, rows, lanes = z_ref.shape
    me = lax.axis_index("dom")
    backed_up(
        plan, reach, width, plan_ref, w_ref, part_ref,
        (got1, got2, got3, got4, got5), all_ref, ext_ref, sum_ref,
    )
    dest = goal_of(plan, plan_ref, rows, lanes)
    for k in range(blocks):
        z_ref[k] = with_goal(k, blocks, growth_ref, sum_ref, dest, me)
    send_items(
        pairs_ref, ends_ref, reach, 1,
        send_slots(width, lambda o, m: z_ref[plan_ref[plan.send + o * width + m]]),
    )


def far_flows(plan, plan_ref, w_ref, split_ref, flow_ref):
    for k in range(plan.slots + 1):
        flow_ref[k] = jnp.zeros(flow_ref.shape[1:], jnp.float32)
    count = plan_ref[plan.far]
    for k in range(plan.slots):
        slot = plan_ref[plan.far_c + k] - plan.blocks
        into = jnp.where(k < count, slot, plan.slots)
        flow_ref[into] = flow_ref[into] + product(
            split_ref[plan_ref[plan.far_r + k]], w_ref[plan_ref[plan.far_t + k]], NN
        )


def turn_kernel(
    plan, reach, width, plan_ref, w_ref, part_ref, growth_ref,
    got1, got2, got3, got4, got5, start_ref,
    z_ref, next_ref, pairs_ref, ends_ref, all_ref, ext_ref, sum_ref, flow_ref,
):
    blocks = plan.blocks
    _, rows, lanes = part_ref.shape
    me = lax.axis_index("dom")
    backed_up(
        plan, reach, width, plan_ref, w_ref, part_ref,
        (got1, got2, got3, got4, got5), all_ref, ext_ref, sum_ref,
    )
    dest = goal_of(plan, plan_ref, rows, lanes)
    for k in range(blocks):
        z = with_goal(k, blocks, growth_ref, sum_ref, dest, me)
        span = slice(k * lanes, (k + 1) * lanes)
        z_ref[k] = z
        store_split(next_ref, k, growth_ref[k] * start_ref[:, span].astype(jnp.float32) / z)
    far_flows(plan, plan_ref, w_ref, next_ref, flow_ref)
    send_items(
        pairs_ref, ends_ref, reach, -1, send_slots(width, lambda o, m: flow_ref[o * width + m])
    )


def flows(
    plan, count, reach, width, plan_ref, w_ref, growth_ref, sum_ref, parts,
    u_ref, next_ref, all_ref, flow_ref,
):
    blocks, rows, _ = u_ref.shape
    me = lax.axis_index("dom")
    for k in range(blocks):
        u_ref[k] = sum_ref[k]
    collect(all_ref, parts)
    for o, f in enumerate(offsets(reach)):
        there = present(me, count, f)
        at = place(me, -f)
        for m in range(width):
            b = plan_ref[plan.send + o * width + m]
            piece = all_ref[at, m * rows : (m + 1) * rows]
            u_ref[b] = u_ref[b] + jnp.where(there, piece, 0.0)
    for k in range(blocks):
        store_split(next_ref, k, growth_ref[k] * u_ref[k])
    far_flows(plan, plan_ref, w_ref, next_ref, flow_ref)


def spread_kernel(
    plan, count, reach, width, plan_ref, w_ref, growth_ref, sum_ref,
    got1, got2, got3, got4, got5,
    u_ref, next_ref, pairs_ref, ends_ref, all_ref, flow_ref,
):
    flows(
        plan, count, reach, width, plan_ref, w_ref, growth_ref, sum_ref,
        (got1, got2, got3, got4, got5), u_ref, next_ref, all_ref, flow_ref,
    )
    send_items(
        pairs_ref, ends_ref, reach, -1, send_slots(width, lambda o, m: flow_ref[o * width + m])
    )


def last_kernel(
    plan, count, reach, width, plan_ref, w_ref, growth_ref, sum_ref,
    got1, got2, got3, got4, got5, z1_got, z2_got, z3_got, z4_got, z5_got,
    u_ref, next_ref, pairs_ref, ends_ref, all_ref, flow_ref, far_ref,
):
    rows = u_ref.shape[1]
    me = lax.axis_index("dom")
    flows(
        plan, count, reach, width, plan_ref, w_ref, growth_ref, sum_ref,
        (got1, got2, got3, got4, got5), u_ref, next_ref, all_ref, flow_ref,
    )
    collect(far_ref, (z1_got, z2_got, z3_got, z4_got, z5_got))
    row = lax.broadcasted_iota(jnp.int32, ends_ref.shape[1:], 0)

    def item(o, ref, where):
        at = place(me, offset_of(o, reach))
        sums = jnp.zeros(ends_ref.shape[1:], jnp.float32)
        for m in range(width):
            lost = far_ref[at, m * rows : (m + 1) * rows] * flow_ref[o * width + m]
            sums = jnp.where(row == m, jnp.sum(lost, axis=0, keepdims=True), sums)
        ref[where] = sums

    send_items(pairs_ref, ends_ref, reach, -1, item)


def node_kernel(
    plan, plan_ref, w_ref, split_ref, z0_ref, z1_ref, z2_ref, u1_ref, u2_ref, visit_ref,
    node_ref, sum_ref,
):
    blocks, _, lanes = z0_ref.shape
    near_products(plan, plan_ref, w_ref, split_ref, sum_ref, False)
    for k in range(blocks):
        left = (
            visit_ref[:, k * lanes : (k + 1) * lanes].astype(jnp.float32)
            - z2_ref[k] * u1_ref[k]
            - z1_ref[k] * u2_ref[k]
            - z0_ref[k] * sum_ref[k]
        )
        node_ref[k] = jnp.sum(left, axis=0, keepdims=True)


def add_gradients(items, act_ref, f_ref, grad, out_sum, bias_sum):
    group = 8
    for c in range(0, len(items), group):
        highs = []
        lows = []
        for at, node in items[c : c + group]:
            act = act_ref[:, at]
            weighted = act * node
            pre = node - weighted * act
            out_sum = out_sum + weighted
            bias_sum = bias_sum + pre
            high = pre.astype(jnp.bfloat16)
            highs.append(high)
            lows.append((pre - high.astype(jnp.float32)).astype(jnp.bfloat16))
        f = jnp.concatenate([f_ref[at] for at, _ in items[c : c + group]], axis=0)
        grad = grad + lax.dot_general(
            jnp.concatenate(highs, axis=1), f, NN, preferred_element_type=jnp.float32
        )
        grad = grad + lax.dot_general(
            jnp.concatenate(lows, axis=1), f, NN, preferred_element_type=jnp.float32
        )
    return grad, out_sum, bias_sum


def own_gradient_kernel(scale, f_ref, act_ref, node_ref, grad_ref, out_ref, bias_ref):
    blocks, _, lanes = node_ref.shape
    items = [
        (slice(k * lanes, (k + 1) * lanes), node_ref[k] * scale) for k in range(blocks)
    ]
    zeros = [jnp.zeros(ref.shape, jnp.float32) for ref in (grad_ref, out_ref, bias_ref)]
    grad_ref[...], out_ref[...], bias_ref[...] = add_gradients(items, act_ref, f_ref, *zeros)


def gradient_kernel(
    plan, count, reach, width, scale, plan_ref, v_ref, f_ref, act_ref, grad_ref, out_ref, bias_ref,
    got1, got2, got3, got4, got5, packed_ref, all_ref,
):
    hidden, lanes = out_ref.shape
    me = lax.axis_index("dom")
    collect(all_ref, (got1, got2, got3, got4, got5))
    items = []
    for o, f in enumerate(offsets(reach)):
        there = present(me, count, f)
        at = place(me, -f)
        for m in range(width):
            block = plan_ref[plan.send + o * width + m]
            row = jnp.where(there, -scale * all_ref[at, m : m + 1], 0.0)
            items.append((pl.ds(pl.multiple_of(block * lanes, lanes), lanes), row))
    grad, out_sum, bias_sum = add_gradients(
        items, act_ref, f_ref, grad_ref[...], out_ref[...], bias_ref[...]
    )
    v = v_ref[...]
    core = me & 1
    half = packed_ref.shape[1]
    parts = hidden // lanes
    tall = hidden * f_ref.shape[1] // lanes

    def put(at, rows):
        packed_ref[jnp.bitwise_xor(core, at // half), at % half : at % half + rows.shape[0]] = rows

    for j in range(parts):
        span = slice(j * lanes, (j + 1) * lanes)
        turned = grad[span].T * v[:, span]
        for i in range(f_ref.shape[1] // 8):
            put((i * parts + j) * 8, turned[i * 8 : (i + 1) * 8])
    ones = jnp.ones((8, lanes), jnp.float32)
    across = lambda x: lax.dot_general(
        ones, x, NT, precision=lax.Precision.HIGHEST, preferred_element_type=jnp.float32
    )[:1]
    bias, out = across(bias_sum) * v, across(out_sum)
    cut = lambda x: [x[:, j * lanes : (j + 1) * lanes] for j in range(parts)]
    put(tall, jnp.concatenate(cut(bias) + cut(out), axis=0))
    for at in range(tall + 2 * parts, 2 * half, 8):
        put(at, jnp.zeros((8, lanes), jnp.float32))


def finish_kernel(mine_ref, other_ref, grad_hbm, bias_hbm, out_hbm, both_ref, bias_ref, out_ref, sem):
    half = mine_ref.shape[0]
    tall, parts = grad_hbm.shape[0], bias_hbm.shape[0]
    core = lax.axis_index("dom") & 1
    both_ref[core] = mine_ref[...]
    both_ref[1 - core] = other_ref[...]
    which, at = tall // half, tall % half
    bias_ref[...] = both_ref[which, at : at + parts]
    out_ref[...] = both_ref[which, at + parts : at + 2 * parts]
    pieces = [(bias_ref, bias_hbm), (out_ref, out_hbm)]
    for h in range(2):
        start, stop = h * half, min((h + 1) * half, tall)
        if start < stop:
            pieces.append((both_ref.at[h, : stop - start], grad_hbm.at[start:stop]))
    copies = [pltpu.make_async_copy(src, dst, sem.at[k]) for k, (src, dst) in enumerate(pieces)]
    for copy in copies:
        copy.start()
    for copy in copies:
        copy.wait()


def values_kernel(z_ref, values_ref):
    blocks, _, lanes = z_ref.shape
    for k in range(blocks):
        values_ref[:, k * lanes : (k + 1) * lanes] = jnp.log(z_ref[k])


def local(
    features, w_input, b_input, w_output, terminal, start_counts, visit_counts, dest_nodes,
    tile_rows, tile_cols, send_blocks, tile_weight,
):
    f32, bf16 = jnp.float32, jnp.bfloat16
    nodes, feat = features.shape
    tiles, lanes, _ = tile_weight.shape
    blocks = nodes // lanes
    rows = terminal.shape[0]
    hidden = w_input.shape[1]
    reach = send_blocks.shape[0] // 2
    width = send_blocks.shape[1]
    slots = 2 * reach * width
    count = lax.axis_size("dom")
    assert reach == 4 and count % 8 == 0
    shape = lambda *s: jax.ShapeDtypeStruct(s, f32)
    row_v = w_output[None, :]

    plan = Plan(blocks, tiles, slots, rows)
    like = lambda x: jax.ShapeDtypeStruct(x.shape, x.dtype)
    field = shape(blocks, rows, lanes)
    padded = shape(blocks + 1, rows, lanes)
    halves = jax.ShapeDtypeStruct((blocks, 2 * rows, lanes), bf16)
    parcels = (shape(3, 2, width * rows, lanes), shape(2, width * rows, lanes))
    smalls = (shape(3, 2, 8, lanes), shape(2, 8, lanes))
    all_s = pltpu.VMEM((PLACES, width * rows, lanes), f32)
    ext_s = pltpu.VMEM((slots, 2 * rows, lanes), bf16)
    sum_s = pltpu.VMEM((blocks + 1, rows, lanes), f32)
    flow_s = pltpu.VMEM((slots + 1, rows, lanes), f32)
    bind = lambda kernel, *lead: functools.partial(kernel, *lead, reach, width)
    flops = 2 * tiles * lanes * lanes * 2 * rows
    moved = tiles * lanes * lanes * 2
    send_t = send_blocks.T
    row_b = b_input[None, :]

    z0, pairs, ends = call(
        bind(first_kernel),
        (field, *parcels),
        [
            pltpu.SMEM(send_t.shape, jnp.int32),
            pltpu.VMEM(terminal.shape, f32),
            pltpu.SemaphoreType.DMA((4,)),
            pltpu.SemaphoreType.DMA,
        ],
        (),
        (),
        flops,
        moved,
        hbm=(send_t, terminal),
    )

    def load():
        return call(
            functools.partial(load_kernel, plan),
            (
                jax.ShapeDtypeStruct((plan.size, lanes), jnp.int32),
                *map(like, (tile_weight, features, w_input, row_b, row_v)),
            ),
            [
                pltpu.SMEM((plan.size,), jnp.int32),
                pltpu.SMEM(tile_rows.shape, jnp.int32),
                pltpu.SMEM(tile_cols.shape, jnp.int32),
                pltpu.SMEM(send_t.shape, jnp.int32),
                pltpu.SMEM(dest_nodes.shape, jnp.int32),
                pltpu.SemaphoreType.DMA((5,)),
                pltpu.SemaphoreType.DMA((4,)),
            ],
            (),
            (),
            flops,
            moved,
            hbm=(tile_rows, tile_cols, send_t, dest_nodes, tile_weight, features, w_input, row_b, row_v),
            after=(ends,),
        )

    far, (plans, weight, feature, w_in, b_in, v_out) = exchange(pairs, ends, load)

    def near(split, forward):
        kernel = functools.partial(near_kernel, plan, forward)
        return call(kernel, padded, [], (plans,), (weight, split), flops, moved)

    act, growth = call(
        network_kernel,
        (shape(hidden, nodes), shape(blocks, 1, lanes)),
        [],
        (),
        (w_in, b_in, v_out, feature),
        2 * nodes * hidden * feat,
        nodes * hidden * 4,
    )

    def near_values(z):
        kernel = functools.partial(near_values_kernel, plan)
        scratch = [pltpu.VMEM((blocks, 2 * rows, lanes), bf16)]
        return call(kernel, padded, scratch, (plans,), (weight, z), flops, moved)

    def backup(part, got):
        return call(
            bind(backup_kernel, plan),
            (field, *parcels),
            [all_s, ext_s, sum_s],
            (plans,),
            (weight, part, growth, *got),
            flops,
            moved,
        )

    z1, pairs, ends = backup(near_values(z0), far)
    got, part = exchange(pairs, ends, lambda: near_values(z1))
    z2, pairs, ends = backup(part, got)
    got, part = exchange(pairs, ends, lambda: near_values(z2))
    z3, split3, pairs, ends = call(
        bind(turn_kernel, plan),
        (field, halves, *parcels),
        [all_s, ext_s, sum_s, flow_s],
        (plans,),
        (weight, part, growth, *got, start_counts),
        2 * flops,
        moved,
    )
    values = call(values_kernel, shape(rows, nodes), [], (), (z3,), flops // 8, nodes * rows * 8)
    got, part = exchange(pairs, ends, lambda: near(split3, False))
    u1, split4, pairs, ends = call(
        bind(spread_kernel, plan, count),
        (field, halves, *parcels),
        [all_s, flow_s],
        (plans,),
        (weight, growth, part, *got),
        flops,
        moved,
    )
    got, part = exchange(pairs, ends, lambda: near(split4, False))
    u2, split5, pairs, ends = call(
        bind(last_kernel, plan, count),
        (field, halves, *smalls),
        [all_s, flow_s, all_s],
        (plans,),
        (weight, growth, part, *got, *far),
        flops,
        moved,
    )
    got, node = exchange(
        pairs,
        ends,
        lambda: call(
            functools.partial(node_kernel, plan),
            shape(blocks, 1, lanes),
            [sum_s],
            (plans,),
            (weight, split5, z0, z1, z2, u1, u2, visit_counts),
            flops,
            moved,
        ),
    )
    every = ("dest", "dom")
    members = count * lax.axis_size("dest")
    tall = hidden * feat // lanes
    share = -(-(tall + 2 * hidden // lanes) // members)
    half = share * members // 2
    scale = 1.0 / math.sqrt(nodes * count * rows * lax.axis_size("dest"))
    own = call(
        functools.partial(own_gradient_kernel, scale),
        (shape(hidden, feat), shape(hidden, lanes), shape(hidden, lanes)),
        [],
        (),
        (feature, act, node),
        4 * nodes * hidden * feat,
        nodes * hidden * 4,
    )
    packed = call(
        functools.partial(gradient_kernel, plan, count, reach, width, scale),
        shape(2, half, lanes),
        [pltpu.VMEM((PLACES, 8, lanes), f32)],
        (plans,),
        (v_out, feature, act, *own, *got),
        4 * slots * lanes * hidden * feat,
        slots * lanes * hidden * 4,
    )
    twins = [(i, i ^ 1) for i in range(count)]
    mine = packed[0] + lax.ppermute(packed[1], "dom", twins)
    same_core = [[i for i in range(members) if i % 2 == core] for core in range(2)]
    swap = lambda x: lax.all_to_all(x, every, 0, 0, tiled=True, axis_index_groups=same_core)
    mine = mine.reshape(members // 2, 1, share * lanes)
    mine = jnp.broadcast_to(swap(mine).sum(axis=0, keepdims=True), mine.shape)
    mine = swap(mine).reshape(half, lanes)
    other = lax.ppermute(mine, "dom", twins)
    in_hbm = pl.BlockSpec(memory_space=pltpu.HBM)
    in_vmem = pl.BlockSpec(memory_space=pltpu.VMEM)
    parts = hidden // lanes
    grad, bias, out = pl.pallas_call(
        finish_kernel,
        out_shape=(shape(tall, lanes), shape(parts, lanes), shape(parts, lanes)),
        in_specs=[in_vmem] * 2,
        out_specs=[in_hbm] * 3,
        scratch_shapes=[
            pltpu.VMEM((2, half, lanes), f32),
            pltpu.VMEM((parts, lanes), f32),
            pltpu.VMEM((parts, lanes), f32),
            pltpu.SemaphoreType.DMA((4,)),
        ],
        compiler_params=pltpu.CompilerParams(vmem_limit_bytes=VMEM_GRANT),
    )(mine, other)
    grad = grad.reshape(feat // 8, parts, 8, lanes).transpose(0, 2, 1, 3).reshape(feat, hidden)
    return values, grad, bias.reshape(-1), out.reshape(-1)


def solution(mesh):
    in_specs = (
        P("dom", None),
        P(),
        P(),
        P(),
        P("dest", "dom"),
        P("dest", "dom"),
        P("dest", "dom"),
        P("dest"),
        P("dom"),
        P("dom"),
        P("dom", None),
        P("dom", None, None),
    )
    out_specs = (P("dest", "dom"), P(), P(), P())
    return jax.shard_map(local, mesh=mesh, in_specs=in_specs, out_specs=out_specs, check_vma=False)
```
